32 devices in a mesh: grp: 2 (over y), seq: 4 (over z), usr: 4 (over x, core).
Axes of the slice: x: 2, y: 2, z: 4, core: 2. Of those that a mesh axis runs over, the one named last changes fastest.
Arguments:
- history_kv: bfloat16 [16, 2048, 768], P(('grp', 'usr'), 'seq'), parts along dimension 0, may hold values from -6 to 6
- candidates: bfloat16 [16, 512, 768], P(('grp', 'usr'), 'seq'), parts along dimension 0, may hold values from -6 to 6
- lengths: int32 [16], P(('grp', 'usr')), parts along dimension 0, may hold values from 256 to 2048, as said below
- w_query: bfloat16 [768, 384], replicated, may hold values from -0.21875 to 0.21875
- w_gate: bfloat16 [768, 384], replicated, may hold values from -0.21875 to 0.21875
- token_mix: bfloat16 [512, 512], P('seq'), may hold values from -0.25 to 0.25
- w_out: bfloat16 [384, 768], replicated, may hold values from -0.3125 to 0.3125
- w_up: bfloat16 [768, 2048], P(None, 'usr'), may hold values from -0.21875 to 0.21875
- w_down: bfloat16 [2048, 768], P('usr'), may hold values from -0.125 to 0.125
Outputs:
- ranked: bfloat16 [16, 512, 768], P(('grp', 'usr'), 'seq'), parts along dimension 0
The draws below stay inside these ranges and needn't reach their ends.
There are 2 independent parts, one for each index of `grp`. The reference program is written for one: setup_inputs(seed, part) draws one part's arguments, and reference() takes and returns one part's arrays. A program takes and returns all parts, laid end to end along the dimension named above; an argument that names none is the same for every part. Nothing has to cross between parts.
Inputs may be any that keep to these rules, and one draw needn't show every extreme that they name: lengths[u] counts the first valid slots of user u's history; in every draw one user has exactly 2048 and another exactly 256.
All inputs are finite; a program needn't handle non-finite values.
Results may differ from the reference program's by a relative error of at most 0.008.
Values may be sent and summed in bfloat16 or wider, within the bound.
A program may use at most 64 MiB of HBM per device.

```python
import math
import jax
import jax.numpy as jnp
from jax import lax

D = 768
HEADS = 3
DH = 128
FF = 2048
CANDS = 512
INNER = 384
USERS = 8
HIST = 2048


def draw_lengths(key, part):
    keys = jax.random.split(key, 2)
    drawn = jax.random.randint(keys[0], (USERS,), HIST // 8, HIST + 1, dtype=jnp.int32)
    order = jax.random.permutation(keys[1], jnp.arange(USERS, dtype=jnp.int32))
    positions = jnp.arange(USERS, dtype=jnp.int32)
    drawn = jnp.where(positions == order[0], HIST, drawn)
    drawn = jnp.where(positions == order[1], HIST // 8, drawn)
    return drawn.astype(jnp.int32)


def level_of(rng, extent, shards, low, top_value):
    level = 1.0
    for position, parts in shards:
        heights = jax.random.uniform(jax.random.fold_in(jax.random.fold_in(rng, 6), position), (parts,), jnp.float32, low / len(shards), top_value / len(shards))
        level = level * jnp.repeat(jnp.exp(heights), extent[position] // parts).reshape((-1,) + (1,) * (len(extent) - 1 - position))
    return level


def normal_values(key, dims, deviation, bound, shards=(), held_as=jnp.bfloat16):
    factor_of = level_of(key, dims, shards, -0.22, 0.18) if shards else 1.0
    values = jax.random.normal(key, dims, jnp.float32) * deviation * factor_of
    return jnp.minimum(jnp.maximum(values, -bound), bound).astype(held_as)


def setup_inputs(seed: int = 0, part: int = 0) -> dict:
    key_of = jax.random.split(jax.random.key(seed), 10)
    part_keys = jax.random.split(jax.random.fold_in(key_of[9], part), 10)
    history_kv = normal_values(part_keys[0], (USERS, HIST, 2 * INNER), 1.0, 6.0, ((0, 4), (1, 4)))
    candidates = normal_values(part_keys[1], (USERS, CANDS, D), 1.0, 6.0, ((0, 4), (1, 4)))
    lengths = draw_lengths(jax.random.fold_in(jax.random.fold_in(key_of[9], part), 71), part)
    w_query = normal_values(key_of[3], (D, INNER), D ** -0.5, 0.21875)
    w_gate = normal_values(key_of[4], (D, INNER), D ** -0.5, 0.21875)
    token_mix = normal_values(key_of[5], (CANDS, CANDS), CANDS ** -0.5, 0.25, ((0, 4),))
    w_out = normal_values(key_of[6], (INNER, D), INNER ** -0.5, 0.3125)
    w_up = normal_values(key_of[7], (D, FF), D ** -0.5, 0.21875, ((1, 4),))
    w_down = normal_values(key_of[8], (FF, D), FF ** -0.5, 0.125, ((0, 4),))
    return dict(history_kv=history_kv, candidates=candidates, lengths=lengths, w_query=w_query, w_gate=w_gate, token_mix=token_mix, w_out=w_out, w_up=w_up, w_down=w_down)


def rounded(values):
    return lax.optimization_barrier(values.astype(jnp.bfloat16)).astype(jnp.float32)

def layer_norm(values):
    center = values - lax.optimization_barrier(jnp.mean(values, axis=-1, keepdims=True))
    spread = lax.optimization_barrier(jnp.mean(center * center, axis=-1, keepdims=True))
    return center * lax.rsqrt(spread + 1e-05)

def reference(history_kv, candidates, lengths, w_query, w_gate, token_mix, w_out, w_up, w_down):
    inner = HEADS * DH
    scale = 1.0 / math.sqrt(DH)
    cand_f = candidates.astype(jnp.float32)
    queries = rounded(jnp.einsum('ucd,de->uce', cand_f, w_query.astype(jnp.float32)))
    block_len = math.gcd(HIST, 2048)
    block_count = HIST // block_len

    def one_user(operands):
        query_rows, cache, limit = operands
        query_heads = query_rows.reshape(CANDS, HEADS, DH)
        blocks = cache.reshape(block_count, block_len, 2 * inner)
        starts = jnp.arange(block_count, dtype=jnp.int32) * block_len

        def step(summed, item):
            block, start = item
            key_heads = block[:, :inner].astype(jnp.float32).reshape(block_len, HEADS, DH)
            value_heads = block[:, inner:].astype(jnp.float32).reshape(block_len, HEADS, DH)
            scores = jnp.einsum('chd,thd->hct', query_heads, key_heads) * scale
            positions = start + jnp.arange(block_len, dtype=jnp.int32)
            visible = positions < limit
            weights = rounded(jnp.where(visible[None, None, :], jax.nn.silu(scores), 0.0))
            contrib = jnp.einsum('hct,thd->chd', weights, value_heads).reshape(CANDS, inner)
            return (summed + contrib, None)
        summed, _ = lax.scan(step, jnp.zeros((CANDS, inner), jnp.float32), (blocks, starts))
        return summed
    attended = lax.map(one_user, (queries, history_kv, lengths))
    normed = rounded(layer_norm(attended))
    mixed = normed + jnp.einsum('cp,upe->uce', token_mix.astype(jnp.float32), normed)
    gate_values = jax.nn.silu(jnp.einsum('ucd,de->uce', cand_f, w_gate.astype(jnp.float32)))
    gated = rounded(mixed * gate_values)
    state = cand_f + jnp.einsum('uce,ed->ucd', gated, w_out.astype(jnp.float32))
    ffn_in = rounded(layer_norm(state))
    hidden = rounded(jax.nn.gelu(jnp.einsum('ucd,df->ucf', ffn_in, w_up.astype(jnp.float32))))
    ranked = state + jnp.einsum('ucf,fd->ucd', hidden, w_down.astype(jnp.float32))
    return ranked.astype(jnp.bfloat16)
```

```python
import functools
import math

import jax
import jax.numpy as jnp
from jax import lax
from jax.experimental import pallas as pl
from jax.experimental.pallas import tpu as pltpu
from jax.sharding import PartitionSpec as P

HEADS = 3
DH = 128
F32 = jnp.float32
BF16 = jnp.bfloat16
MESH = pl.DeviceIdType.MESH
ACROSS_STEPS = (1, 2, 3, 4)
GROUP_STEPS = (3, 4, 5, 6)
MIX_STEP = 0
SHARE_STEPS = (3, 4)
COLUMNS = 256


def layer_norm(values):
    center = values - jnp.mean(values, axis=-1, keepdims=True)
    spread = jnp.mean(center * center, axis=-1, keepdims=True)
    return center * lax.rsqrt(spread + 1e-05)


def silu_of_double(half):
    return half + half * jnp.tanh(half)


def gelu_tanh(v):
    return 0.5 * v * (1.0 + jnp.tanh(math.sqrt(2.0 / math.pi) * (v + 0.044715 * (v * v * v))))


def dot(a, b):
    return jnp.dot(a, b, preferred_element_type=F32)


def kernel(
    seqs,
    kv_hbm, cand_hbm, len_hbm, wq_hbm, wg_hbm, tm_hbm, wo_hbm, wu_hbm, wd_hbm,
    out_ref,
    kv, cand, wq, wg, tm, wo, wu, wd,
    values, queries, sums, outgoing, incoming, normed, mixed_out, mixed_in, gates, states,
    lens, load_sem,
    q_send, q_recv, p_send, p_recv, t_send, t_recv, f_send, m_send, m_recv,
    wo_send, wo_recv, wc_send, wc_recv, wx_send, wx_recv, wy_send, wy_recv,
):
    users, rows, _ = cand.shape
    hist = kv.shape[1]
    inner = wq.shape[1]
    hidden_slots = wu.shape[0]
    g, s, u = lax.axis_index("grp"), lax.axis_index("seq"), lax.axis_index("usr")
    partner = u + 1 - 2 * lax.rem(u, 2)
    across = lax.rem(u + 2, 4)
    across_partner = lax.rem(partner + 2, 4)
    left, right = (g, s - 1, u), (g, s + 1, u)
    has_left, has_right = s > 0, s < seqs - 1

    first_owned = lax.rem(u, 2) * users
    owned = s - first_owned
    is_owner = jnp.logical_and(owned >= 0, owned < users)

    loads = {}
    for index, (name, source, target) in enumerate((
        ("cand", cand_hbm, cand), ("wq", wq_hbm, wq), ("kv", kv_hbm, kv), ("wg", wg_hbm, wg),
        ("tm", tm_hbm, tm.at[s]), ("wo", wo_hbm, wo), ("wu", wu_hbm, wu.at[u]), ("wd", wd_hbm, wd.at[u]), ("lens", len_hbm, lens),
    )):
        loads[name] = pltpu.make_async_copy(source, target, load_sem.at[index])

    for name in ("cand", "wq", "lens"):
        loads[name].start()

    barrier = pltpu.get_barrier_semaphore()
    peers = [(g, s, partner), (g, s, across), (1 - g, s, u)]
    peers += [(g, lax.rem(s + step, seqs), u) for step in range(1, seqs)]
    for peer in peers:
        pl.semaphore_signal(barrier, inc=1, device_id=peer, device_id_type=MESH)

    def remote(source, target, send, recv, device):
        return pltpu.make_async_remote_copy(
            src_ref=source, dst_ref=target, send_sem=send, recv_sem=recv,
            device_id=device, device_id_type=MESH,
        )

    weights = ((wu_hbm, wu), (wd_hbm, wd))

    def rows_of(piece, half):
        size = weights[piece // 2][1].shape[1] // 4
        return pl.ds(pl.multiple_of((half * 2 + piece % 2) * size, size), size)

    def piece_of(piece, slot, half):
        return weights[piece // 2][1].at[slot, rows_of(piece, half)]

    def to_partner_own(w, slot):
        return remote(weights[w][0], weights[w][1].at[slot], wo_send.at[w], wo_recv.at[w], (g, s, partner))

    def to_across(piece, slot):
        source = weights[piece // 2][0].at[rows_of(piece, g)]
        return remote(source, piece_of(piece, slot, g), wx_send.at[piece], wx_recv.at[piece], (g, s, across))

    def to_group(piece, half):
        part = piece_of(piece, across, half)
        return remote(part, part, wy_send.at[piece], wy_recv.at[piece], (1 - g, s, u))

    def to_partner_far(piece, slot, half, which):
        part = piece_of(piece, slot, half)
        return remote(part, part, wc_send.at[piece, which], wc_recv.at[piece, which], (g, s, partner))

    def across_arrived(piece):
        to_across(piece, across).wait_recv()
        to_group(piece, g).start()
        to_partner_far(piece, across, g, 0).start()

    def group_arrived(piece):
        to_group(piece, 1 - g).wait_recv()
        to_partner_far(piece, across, 1 - g, 1).start()

    def gather_copy(buf, send, recv, m, block, way):
        ref = buf.at[m, block]
        return remote(ref, ref, send.at[m, block, way], recv.at[m, block], (left, right)[way])

    def gather_step(buf, send, recv, m, step):
        @pl.when(s >= step)
        def _():
            block = s - step
            gather_copy(buf, send, recv, m, block, 1).wait_recv()

            @pl.when(has_right)
            def _():
                gather_copy(buf, send, recv, m, block, 1).start()

        @pl.when(s + step < seqs)
        def _():
            block = s + step
            gather_copy(buf, send, recv, m, block, 0).wait_recv()

            @pl.when(has_left)
            def _():
                gather_copy(buf, send, recv, m, block, 0).start()

    def gather_own(buf, send, recv, m):
        @pl.when(has_right)
        def _():
            gather_copy(buf, send, recv, m, s, 1).start()

        @pl.when(has_left)
        def _():
            gather_copy(buf, send, recv, m, s, 0).start()

    def gather_finish(buf, send, recv):
        for m in range(users):
            for block in range(seqs):
                @pl.when(jnp.logical_and(block <= s, has_right))
                def _():
                    gather_copy(buf, send, recv, m, block, 1).wait_send()

                @pl.when(jnp.logical_and(block >= s, has_left))
                def _():
                    gather_copy(buf, send, recv, m, block, 0).wait_send()

    loads["cand"].wait()
    loads["wq"].wait()
    for m in range(users):
        queries[m, s] = dot(cand[m], wq[...]).astype(BF16)
        if m == 0:
            pl.semaphore_wait(barrier, len(peers))
        gather_own(queries, q_send, q_recv, m)
    for piece in range(4):
        to_across(piece, u).start()
    for name in ("kv", "wg", "tm", "wo", "wu", "wd"):
        loads[name].start()
    for w in range(2):
        to_partner_own(w, u).start()

    loads["kv"].wait()
    loads["lens"].wait()
    for m in range(users):
        slots = s * hist + lax.broadcasted_iota(jnp.int32, (hist, 1), 0)
        visible = jnp.where(slots < lens[m], 1.0, 0.0)
        values[m] = (kv[m, :, inner:].astype(F32) * visible).astype(BF16)

    half_scale = 0.5 / math.sqrt(DH)

    def attend(m, block):
        for head in range(HEADS):
            cols = slice(head * DH, (head + 1) * DH)
            scores = lax.dot_general(
                queries[m, block, :, cols], kv[m, :, cols], (((1,), (1,)), ((), ())),
                preferred_element_type=F32,
            )
            weight = silu_of_double(scores * half_scale).astype(BF16)
            sums[m, block, :, cols] = dot(weight, values[m, :, cols])

    def partial_copy(m, block, way):
        return remote(
            outgoing.at[m, block], incoming.at[way, m, block],
            p_send.at[m, block], p_recv.at[way, m, block], (left, right)[way],
        )

    def pass_on(m, block, way, first):
        @pl.when(first)
        def _():
            outgoing[m, block] = sums[m, block].astype(BF16)

        @pl.when(jnp.logical_not(first))
        def _():
            partial_copy(m, block, way).wait_recv()
            outgoing[m, block] = (sums[m, block] + incoming[way, m, block].astype(F32)).astype(BF16)

        partial_copy(m, block, way).start()

    chip = lax.div(u, 2)
    quarter = rows // 4

    def quarter_rows(group, near):
        return pl.ds(pl.multiple_of((group * 2 + near) * quarter, quarter), quarter)

    def mix_copy(m):
        return remote(
            tm_hbm.at[quarter_rows(g, chip)], tm.at[s, quarter_rows(g, chip)],
            t_send.at[m], t_recv.at[s, 0], (g, first_owned + m, u),
        )

    def mix_share(block, which):
        part = tm.at[block, quarter_rows(g, 1 - chip if which == 3 else chip)]
        device = (g, s, across) if which == 1 else (1 - g, s, u)
        return remote(part, part, f_send.at[block, which], t_recv.at[block, which], device)

    def mix_arrived(block, which):
        part = tm.at[block, quarter_rows(1 - g if which > 1 else g, 1 - chip if which % 2 else chip)]
        remote(part, part, f_send.at[block, which], t_recv.at[block, which], (1 - g, s, u)).wait_recv()

    def for_far_blocks(do):
        for block in range(seqs):
            @pl.when(jnp.logical_and(is_owner, block != s))
            def _():
                do(block)

    def share_first(block):
        mix_arrived(block, 0)
        mix_share(block, 1).start()
        mix_share(block, 2).start()

    def share_second(block):
        mix_arrived(block, 1)
        mix_share(block, 3).start()

    def share_last(block):
        mix_arrived(block, 2)
        mix_arrived(block, 3)

    def share_sent(block):
        for which in (1, 2, 3):
            mix_share(block, which).wait_send()

    mirror = seqs - 1 - s
    def stage_of(step, m):
        if step < seqs:
            if step > 0:
                gather_step(queries, q_send, q_recv, m, step)

            @pl.when(s >= step)
            def _():
                attend(m, s - step)

            if step > 0:
                @pl.when(s + step < seqs)
                def _():
                    attend(m, s + step)

        owner = first_owned + m
        block = step - s

        @pl.when((owner > s) & (block >= 0) & (block < seqs))
        def _():
            pass_on(m, block, 1, s == 0)

        far = step - mirror

        @pl.when((owner < s) & (far >= 0) & (far < seqs))
        def _():
            pass_on(m, seqs - 1 - far, 0, mirror == 0)

    for step in range(2 * seqs - 2):
        for m in range(users):
            stage_of(step, m)

        if step == 0:
            loads["wg"].wait()
            for m in range(users):
                gates[m] = silu_of_double(dot(cand[m], wg[...]) * 0.5)
        if step == MIX_STEP:
            for m in range(users):
                @pl.when(first_owned + m != s)
                def _():
                    mix_copy(m).start()
        if step == SHARE_STEPS[0]:
            for_far_blocks(share_first)
        if step == SHARE_STEPS[1]:
            for_far_blocks(share_second)
        for piece in range(4):
            if step == ACROSS_STEPS[piece]:
                across_arrived(piece)
            if step == GROUP_STEPS[piece]:
                group_arrived(piece)

    def mixed_copy(block, m):
        return remote(
            mixed_out.at[block], mixed_in.at[m], m_send.at[block], m_recv.at[m], (g, block, u)
        )

    order = sorted(range(seqs), key=lambda block: min(block, seqs - 1 - block))
    loads["tm"].wait()
    @pl.when(is_owner)
    def _():
        for block in range(seqs):
            @pl.when(has_left)
            def _():
                partial_copy(owned, block, 1).wait_recv()
                sums[owned, block] = sums[owned, block] + incoming[1, owned, block].astype(F32)

            @pl.when(has_right)
            def _():
                partial_copy(owned, block, 0).wait_recv()
                sums[owned, block] = sums[owned, block] + incoming[0, owned, block].astype(F32)

            normed[block * rows:(block + 1) * rows] = layer_norm(sums[owned, block]).astype(BF16)
        for_far_blocks(share_last)
        for block in order:
            mixed = normed[block * rows:(block + 1) * rows].astype(F32) + dot(tm[block], normed[...])
            mixed_out[block] = mixed.astype(BF16)

            @pl.when(block != s)
            def _():
                mixed_copy(block, owned).start()

            @pl.when(block == s)
            def _():
                mixed_in[owned] = mixed.astype(BF16)

    for piece in range(4):
        if GROUP_STEPS[piece] >= 2 * seqs - 2:
            group_arrived(piece)
    loads["wo"].wait()
    ffn_ins = []
    for m in range(users):
        @pl.when(first_owned + m != s)
        def _():
            mixed_copy(s, m).wait_recv()

        gated = (mixed_in[m].astype(F32) * gates[m]).astype(BF16)
        state = cand[m].astype(F32) + dot(gated, wo[...])
        states[m * rows:(m + 1) * rows] = state
        ffn_ins.append(layer_norm(state).astype(BF16))
    ffn_in = jnp.concatenate(ffn_ins, axis=0)

    for w in range(2):
        loads[("wu", "wd")[w]].wait()
        to_partner_own(w, partner).wait_recv()
    for piece in range(4):
        to_partner_far(piece, across_partner, g, 0).wait_recv()
        to_partner_far(piece, across_partner, 1 - g, 1).wait_recv()
    width = cand.shape[2]
    hidden = [gelu_tanh(dot(ffn_in, wu[slot])).astype(BF16) for slot in range(hidden_slots)]
    for first in range(0, width, COLUMNS):
        cols = slice(first, min(first + COLUMNS, width))
        total = states[:, cols]
        for slot in range(hidden_slots):
            total = total + dot(hidden[slot], wd[slot, :, cols])
        for m in range(users):
            out_ref[m, :, cols] = total[m * rows:(m + 1) * rows].astype(BF16)

    gather_finish(queries, q_send, q_recv)
    for_far_blocks(share_sent)
    for m in range(users):
        @pl.when(first_owned + m != s)
        def _():
            mix_copy(m).wait_send()
            for block in range(seqs):
                partial_copy(m, block, 1).wait_send()

    @pl.when(is_owner)
    def _():
        for block in range(seqs):
            @pl.when(block != s)
            def _():
                mixed_copy(block, owned).wait_send()

    for w in range(2):
        to_partner_own(w, u).wait_send()
    for piece in range(4):
        to_across(piece, u).wait_send()
        to_group(piece, g).wait_send()
        to_partner_far(piece, across, g, 0).wait_send()
        to_partner_far(piece, across, 1 - g, 1).wait_send()


def fused(seqs, usrs, history_kv, candidates, lengths, w_query, w_gate, token_mix, w_out, w_up, w_down):
    users, hist, _ = history_kv.shape
    rows, width = candidates.shape[1:]
    inner = w_query.shape[1]
    depth = w_up.shape[1]
    dma = pltpu.SemaphoreType.DMA
    hbm = pl.BlockSpec(memory_space=pltpu.HBM)
    operands = (history_kv, candidates, lengths, w_query, w_gate, token_mix, w_out, w_up, w_down)
    return pl.pallas_call(
        functools.partial(kernel, seqs),
        out_shape=jax.ShapeDtypeStruct(candidates.shape, BF16),
        in_specs=[hbm] * len(operands),
        out_specs=pl.BlockSpec(memory_space=pltpu.VMEM),
        scratch_shapes=[
            pltpu.VMEM(history_kv.shape, BF16),
            pltpu.VMEM(candidates.shape, BF16),
            pltpu.VMEM(w_query.shape, BF16),
            pltpu.VMEM(w_gate.shape, BF16),
            pltpu.VMEM((seqs, *token_mix.shape), BF16),
            pltpu.VMEM(w_out.shape, BF16),
            pltpu.VMEM((usrs, width, depth), BF16),
            pltpu.VMEM((usrs, depth, width), BF16),
            pltpu.VMEM((users, hist, inner), BF16),
            pltpu.VMEM((users, seqs, rows, inner), BF16),
            pltpu.VMEM((users, seqs, rows, inner), F32),
            pltpu.VMEM((users, seqs, rows, inner), BF16),
            pltpu.VMEM((2, users, seqs, rows, inner), BF16),
            pltpu.VMEM((seqs * rows, inner), BF16),
            pltpu.VMEM((seqs, rows, inner), BF16),
            pltpu.VMEM((users, rows, inner), BF16),
            pltpu.VMEM((users, rows, inner), F32),
            pltpu.VMEM((users * rows, width), F32),
            pltpu.SMEM(lengths.shape, jnp.int32),
            dma((9,)),
            dma((users, seqs, 2)), dma((users, seqs)),
            dma((users, seqs)), dma((2, users, seqs)),
            dma((users,)), dma((seqs, 4)), dma((seqs, 4)), dma((seqs,)), dma((users,)),
            dma((2,)), dma((2,)), dma((4, 2)), dma((4, 2)),
            dma((4,)), dma((4,)), dma((4,)), dma((4,)),
        ],
        compiler_params=pltpu.CompilerParams(
            collective_id=0, has_side_effects=True, vmem_limit_bytes=34 * 1024 * 1024
        ),
        name="rank_layer",
    )(*(pltpu.with_memory_space_constraint(operand, pltpu.HBM) for operand in operands))


def shards(history_kv, candidates, lengths, w_query, w_gate, token_mix, w_out, w_up, w_down):
    user_count, hist_dev, _ = history_kv.shape
    inner = w_query.shape[1]
    half = hist_dev // 2
    scale = 1.0 / math.sqrt(DH)
    seq_index = lax.axis_index("seq")
    first_start = seq_index * hist_dev
    sections = ((history_kv[:, :half], first_start), (history_kv[:, half:], first_start + half))
    offsets = lax.iota(jnp.int32, half)
    queries = jnp.einsum(
        "ucd,de->uce", candidates, w_query, preferred_element_type=jnp.float32
    ).astype(jnp.bfloat16)
    piece = lax.all_gather(queries, "seq", axis=1, tiled=True)
    row_count = piece.shape[1]
    results = []
    for member in range(user_count):
        query_heads = piece[member].reshape(row_count, HEADS, DH)
        limit = lengths[member]
        summed = jnp.zeros((row_count, inner), jnp.float32)
        for section, section_start in sections:
            key_heads = section[member, :, :inner].reshape(half, HEADS, DH)
            value_heads = section[member, :, inner:].reshape(half, HEADS, DH)

            def compute(
                operand,
                key_heads=key_heads,
                value_heads=value_heads,
                section_start=section_start,
                query_heads=query_heads,
                limit=limit,
            ):
                scores = (
                    jnp.einsum(
                        "chd,thd->hct", query_heads, key_heads, preferred_element_type=jnp.float32
                    )
                    * scale
                )
                visible = section_start + offsets < limit
                weights = jnp.where(visible[None, None, :], jax.nn.silu(scores), 0.0).astype(
                    jnp.bfloat16
                )
                contrib = jnp.einsum(
                    "hct,thd->chd", weights, value_heads, preferred_element_type=jnp.float32
                )
                return contrib.reshape(row_count, inner)

            def skipped(operand):
                return jnp.zeros((row_count, inner), jnp.float32)

            summed = summed + lax.cond(section_start < limit, compute, skipped, 0)
        results.append(summed)
    partial_sums = jnp.stack(results)
    attended = lax.psum_scatter(partial_sums, "seq", scatter_dimension=1, tiled=True)
    normed = layer_norm(attended).astype(jnp.bfloat16)
    mixed = normed.astype(jnp.float32) + jnp.einsum(
        "cp,upe->uce",
        token_mix,
        lax.all_gather(normed, "seq", axis=1, tiled=True),
        preferred_element_type=jnp.float32,
    )
    gate_values = jax.nn.silu(
        jnp.einsum("ucd,de->uce", candidates, w_gate, preferred_element_type=jnp.float32)
    )
    gated = (mixed * gate_values).astype(jnp.bfloat16)
    state = candidates.astype(jnp.float32) + jnp.einsum(
        "uce,ed->ucd", gated, w_out, preferred_element_type=jnp.float32
    )
    ffn_in = layer_norm(state).astype(jnp.bfloat16)
    hidden = jax.nn.gelu(
        jnp.einsum(
            "ucd,df->ucf",
            lax.all_gather(ffn_in, "usr", axis=0, tiled=True),
            w_up,
            preferred_element_type=jnp.float32,
        )
    ).astype(jnp.bfloat16)
    ffn_terms = jnp.einsum("ucf,fd->ucd", hidden, w_down, preferred_element_type=jnp.float32)
    ffn_out = lax.psum_scatter(
        ffn_terms.astype(jnp.bfloat16), "usr", scatter_dimension=0, tiled=True
    ).astype(jnp.float32)
    return (state + ffn_out).astype(jnp.bfloat16)


def solution(mesh):
    sizes = dict(mesh.shape)
    seqs, usrs = sizes["seq"], sizes["usr"]
    def body(history_kv, candidates, *rest):
        operands = (history_kv, candidates, *rest)
        if sizes["grp"] == 2 and usrs == 4 and seqs == 2 * candidates.shape[0] and seqs >= 4:
            return fused(seqs, usrs, *operands)
        return shards(*operands)

    return jax.shard_map(
        body,
        mesh=mesh,
        in_specs=(
            P(("grp", "usr"), "seq", None),
            P(("grp", "usr"), "seq", None),
            P(("grp", "usr")),
            P(),
            P(),
            P("seq", None),
            P(),
            P(None, "usr"),
            P("usr", None),
        ),
        out_specs=P(("grp", "usr"), "seq", None),
        check_vma=False,
    )
```

```python
import functools
import math

import jax
import jax.numpy as jnp
from jax import lax
from jax.experimental import pallas as pl
from jax.experimental.pallas import tpu as pltpu
from jax.sharding import PartitionSpec as P

HEADS = 3
DH = 128
F32 = jnp.float32
BF16 = jnp.bfloat16
MESH = pl.DeviceIdType.MESH
COLUMNS = 256
PIECES = 4
DEPTH = 2

(ATTEND, ARRIVED, PASS, SEND_SUM, COMPLETE, PIECE_ACROSS, PIECE_GROUP, SEND_MIX, PASS_MIX, PREMIX, MIX,
 SHARE_FIRST, SHARE_SECOND) = range(1, 14)
PLAN = (
    (
        (
            3001, 1000, 3102, 8000, 1100, 4101, 2110, 1110, 4111, 6000, 2010, 1010, 3101, 6001, 7000,
            6002, 7001, 6003, 12000, 7002, 6004, 7003, 2130, 1130, 6005, 4131, 2120, 1120, 13000, 4121,
            2020, 1020, 7004, 2030, 1030, 6006, 5030, 7005, 6007, 5000, 5020, 10000, 5010, 11000, 7006,
            7007,
        ),
        (
            3110, 3112, 3010, 1010, 4010, 1110, 3012, 2120, 1120, 6000, 2000, 3003, 1000, 4000, 6001,
            9000, 12000, 2130, 3130, 1130, 6002, 7000, 3120, 3002, 7001, 2020, 3020, 1020, 6003, 2100,
            1100, 13000, 7002, 2030, 3030, 1030, 6004, 4030, 7003, 6005, 4020, 5130, 5110, 6006, 7004,
            6007, 5120, 10000, 5100, 11000, 7005, 7006, 7007,
        ),
        (
            3121, 3123, 1120, 8000, 1020, 3023, 2130, 2110, 3131, 3113, 1130, 6000, 1110, 3021, 2100,
            3103, 1100, 4131, 6001, 2010, 3013, 1010, 6002, 7000, 6003, 7001, 2030, 3031, 1030, 4031,
            6004, 7002, 4121, 2000, 1000, 4021, 6005, 7003, 4111, 4000, 6006, 7004, 4101, 4010, 6007,
            7005, 7006, 7007,
        ),
        (
            3132, 1130, 4132, 8000, 1030, 4032, 6000, 3032, 2120, 1120, 4122, 6001, 2020, 1020, 4022,
            6002, 7000, 2110, 1110, 4112, 7001, 6003, 2000, 1000, 4002, 2100, 1100, 4102, 6004, 7002,
            2010, 1010, 4012, 7003, 6005, 7004, 6006, 7005, 6007, 7006, 7007,
        ),
    ),
    (
        (
            3001, 1000, 3102, 8000, 1100, 4101, 2010, 1010, 6000, 6001, 7000, 3101, 6002, 7001, 6003,
            7002, 6004, 12000, 2110, 1110, 6005, 4111, 7003, 2020, 1020, 2120, 1120, 4121, 7004, 6006,
            2130, 1130, 4131, 5020, 13000, 6007, 7005, 5010, 2030, 1030, 7006, 5030, 10000, 5000, 11000,
            7007,
        ),
        (
            3010, 1110, 3013, 1010, 4010, 3112, 2000, 1000, 4000, 6000, 3002, 3012, 6001, 2020, 1020,
            6002, 7000, 9000, 12000, 3110, 3020, 6003, 7001, 2100, 1100, 2120, 3120, 1120, 6004, 7002,
            2130, 3130, 1130, 13000, 4020, 6005, 7003, 2030, 3030, 1030, 5110, 6006, 7004, 4030, 6007,
            5130, 5120, 10000, 5100, 11000, 7005, 7006, 7007,
        ),
        (
            1020, 4021, 1120, 3021, 3023, 8000, 6000, 3123, 2110, 3113, 1110, 4111, 6001, 2100, 3103,
            1100, 7000, 6002, 3121, 2000, 3003, 1000, 6003, 2130, 3131, 1130, 7001, 4131, 2010, 1010,
            6004, 2030, 3031, 1030, 4031, 7002, 4010, 6005, 7003, 4121, 6006, 7004, 4101, 6007, 7005,
            4000, 7006, 7007,
        ),
        (
            1030, 8000, 4032, 1130, 4132, 3132, 6000, 3032, 2010, 1010, 4012, 2020, 1020, 6001, 4021,
            7000, 6002, 2120, 1120, 4122, 7001, 2110, 1110, 6003, 4111, 7002, 6004, 2100, 1100, 4102,
            7003, 2000, 1000, 6005, 4002, 7004, 6006, 7005, 6007, 7006, 7007,
        ),
    ),
)
QUERY_ORDER = (((0, 1), (0, 1), (0, 1), (0, 1)), ((0, 1), (0, 1), (0, 1), (0, 1)))
TAIL_ORDER = (((0, 1), (1, 0), (1, 0), (1, 0)), ((0, 1), (1, 0), (1, 0), (1, 0)))


def numbers_of(step):
    return step // 100 % 10, step // 10 % 10, step % 10


def steps_of(odd, k, kind):
    return [numbers_of(t) for t in PLAN[odd][k] if t // 1000 == kind]


def children(odd, k, m, b):
    return [j for j in range(len(PLAN[odd])) if (m, b, k) in steps_of(odd, j, SEND_SUM)]


def lanes_of(m):
    places = range(len(PLAN[0]))
    return max(len(children(odd, k, m, b)) for odd in range(2) for k in places for b in places)


def layer_norm(values):
    center = values - jnp.mean(values, axis=-1, keepdims=True)
    spread = jnp.mean(center * center, axis=-1, keepdims=True)
    return center * lax.rsqrt(spread + 1e-05)


def silu_of_double(half):
    return half + half * jnp.tanh(half)


def gelu_tanh(v):
    return 0.5 * v * (1.0 + jnp.tanh(math.sqrt(2.0 / math.pi) * (v + 0.044715 * (v * v * v))))


def dot(a, b):
    return jnp.dot(a, b, preferred_element_type=F32)


def kernel(
    seqs,
    kv_hbm, cand_hbm, len_hbm, wq_hbm, wg_hbm, tm_hbm, wo_hbm, wu_hbm, wd_hbm,
    out_ref,
    kv, cand, wq, wg, tm, wo, wu, wd,
    values, queries, sums, outgoing, incoming, normed, mixed_sum, mixed_out, mixed_in, gates, states,
    lens, load_sem,
    q_send, q_recv, p_send, p_recv, t_send, t_recv, f_send, m_send, m_recv,
    w_send, wo_recv, wx_recv, wy_recv, wc_recv, far,
):
    users, rows, width = cand.shape
    hist = kv.shape[1]
    inner = wq.shape[1]
    g, s, u = lax.axis_index("grp"), lax.axis_index("seq"), lax.axis_index("usr")
    odd = lax.rem(u, 2)
    partner = u + 1 - 2 * odd
    across = lax.rem(u + 2, 4)
    across_partner = lax.rem(partner + 2, 4)
    step = 1 - 2 * odd
    place = s + odd * (seqs - 1 - 2 * s)

    def user_of(m):
        return m + odd * (users - 1 - 2 * m)

    def block_of(b):
        return b + odd * (seqs - 1 - 2 * b)

    def at_place(b):
        return (g, block_of(b), u)

    variants = [(c, k) for c in range(2) for k in range(seqs)]
    variant = odd * seqs + place

    def pick(choices):
        if len(set(choices)) == 1:
            return choices[0]
        value = choices[-1]
        for v in range(len(choices) - 1):
            value = jnp.where(variant == v, choices[v], value)
        return value

    def by_variant(do):
        for v, (c, k) in enumerate(variants):
            @pl.when(variant == v)
            def _():
                do(c, k)

    loads = {}
    for index, (name, source, target) in enumerate((
        ("cand", cand_hbm, cand), ("wq", wq_hbm, wq), ("lens", len_hbm, lens), ("kv", kv_hbm, kv), ("wg", wg_hbm, wg),
        ("tm", tm_hbm, tm.at[s]), ("wo", wo_hbm, wo), ("wu", wu_hbm, wu.at[u]), ("wd", wd_hbm, wd.at[u]),
    )):
        loads[name] = pltpu.make_async_copy(source, target, load_sem.at[index])

    for name in ("cand", "wq", "lens"):
        loads[name].start()

    barrier = pltpu.get_barrier_semaphore()
    near = [(g, s, partner), (g, s, across), (1 - g, s, u)]
    for peer in near:
        pl.semaphore_signal(barrier, inc=1, device_id=peer, device_id_type=MESH)

    @pl.when(s > 0)
    def _():
        pl.semaphore_signal(barrier, inc=1, device_id=(g, s - 1, u), device_id_type=MESH)

    @pl.when(s < seqs - 1)
    def _():
        pl.semaphore_signal(barrier, inc=1, device_id=(g, s + 1, u), device_id_type=MESH)

    def remote(source, target, send, recv, device):
        return pltpu.make_async_remote_copy(
            src_ref=source, dst_ref=target, send_sem=send, recv_sem=recv,
            device_id=device, device_id_type=MESH,
        )

    def drain(ref, sem):
        pltpu.make_async_copy(ref, ref, sem).wait()

    weights = ((wu_hbm, wu), (wd_hbm, wd))

    def rows_of(piece, half):
        size = weights[piece // PIECES][1].shape[1] // (2 * PIECES)
        return pl.ds(pl.multiple_of((half * PIECES + piece % PIECES) * size, size), size)

    def piece_of(piece, slot, half):
        return weights[piece // PIECES][1].at[slot, rows_of(piece, half)]

    def to_partner_own(w):
        return remote(weights[w][0], weights[w][1].at[u], w_send.at[w], wo_recv.at[w], (g, s, partner))

    def to_across(piece, slot):
        w = piece // PIECES
        source = weights[w][0].at[rows_of(piece, g)]
        return remote(source, piece_of(piece, slot, g), w_send.at[w], wx_recv.at[piece], (g, s, across))

    def to_group(piece, half):
        part = piece_of(piece, across, half)
        return remote(part, part, w_send.at[piece // PIECES], wy_recv.at[piece], (1 - g, s, u))

    def to_partner_far(piece, half):
        part = piece_of(piece, across, half)
        w = piece // PIECES
        return remote(part, part, w_send.at[w], wc_recv.at[w], (g, s, partner))

    def across_arrived(piece):
        to_across(piece, across).wait_recv()
        if piece + DEPTH < 2 * PIECES:
            to_across(piece + DEPTH, u).start()
        to_group(piece, g).start()
        to_partner_far(piece, g).start()

    def group_arrived(piece):
        to_group(piece, 1 - g).wait_recv()
        to_partner_far(piece, 1 - g).start()

    def query_copy(m, b, to):
        ref = queries.at[m, b]
        return remote(ref, ref, q_send, q_recv.at[m, b], at_place(to))

    def early(c, k):
        kinds = [t // 1000 for t in PLAN[c][k]]
        ahead = [t for t in PLAN[c][k][:kinds.index(ATTEND)] if t // 1000 == PASS]
        return [t for t in ahead if numbers_of(t)[:2] == (QUERY_ORDER[c][k][0], k) and abs(t % 10 - k) == 1]

    def pass_queries(m, b, to):
        query_copy(m, b, to).start()

    def send_early(c, k):
        for t in early(c, k):
            pass_queries(*numbers_of(t))

    orders = [QUERY_ORDER[c][k] for c, k in variants]
    first, second = pick([o[0] for o in orders]), pick([o[1] for o in orders])
    loads["cand"].wait()
    loads["wq"].wait()
    loads["kv"].start()
    queries[first, place] = dot(cand[user_of(first)], wq[...]).astype(BF16)
    neighbours = (s > 0).astype(jnp.int32) + (s < seqs - 1).astype(jnp.int32)
    pl.semaphore_wait(barrier, len(near) + neighbours)
    by_variant(send_early)
    for piece in range(DEPTH):
        to_across(piece, u).start()
    for way in (-1, 1):
        @pl.when((s + way >= 0) & (s + way < seqs))
        def _():
            pl.semaphore_signal(far, inc=1, device_id=(g, s + way, u), device_id_type=MESH)

    queries[second, place] = dot(cand[user_of(second)], wq[...]).astype(BF16)
    for w in range(2):
        to_partner_own(w).start()
    for name in ("wg", "tm", "wo", "wu", "wd"):
        loads[name].start()

    loads["lens"].wait()
    loads["kv"].wait()
    for m in range(users):
        slots = s * hist + lax.broadcasted_iota(jnp.int32, (hist, 1), 0)
        visible = jnp.where(slots < lens[m], 1.0, 0.0)
        values[m] = (kv[m, :, inner:].astype(F32) * visible).astype(BF16)

    half_scale = 0.5 / math.sqrt(DH)

    def attend(m, b):
        user = user_of(m)
        for head in range(HEADS):
            cols = slice(head * DH, (head + 1) * DH)
            scores = lax.dot_general(
                queries[m, b, :, cols], kv[user, :, cols], (((1,), (1,)), ((), ())),
                preferred_element_type=F32,
            )
            weight = silu_of_double(scores * half_scale).astype(BF16)
            sums[m, b, :, cols] = dot(weight, values[user, :, cols])

    lane_start = [sum(lanes_of(j) for j in range(m)) for m in range(users)]

    def sum_copy(c, source, m, b, to):
        lane = lane_start[m] + children(c, to, m, b).index(source)
        return remote(
            outgoing.at[m, b], incoming.at[lane * seqs + b], p_send, p_recv.at[lane, b], at_place(to)
        )

    def gather_sum(c, k, m, b):
        total = sums[m, b]
        for child in children(c, k, m, b):
            copy = sum_copy(c, child, m, b, k)
            copy.wait_recv()
            lane = lane_start[m] + children(c, k, m, b).index(child)
            total = total + incoming[lane * seqs + b].astype(F32)
        return total

    def send_sum(c, k, m, b, to):
        outgoing[m, b] = gather_sum(c, k, m, b).astype(BF16)
        sum_copy(c, k, m, b, to).start()

    def sum_complete(c, k, m, b):
        first_row = pl.multiple_of(block_of(b) * rows, rows)
        normed[pl.ds(first_row, rows)] = layer_norm(gather_sum(c, k, m, b)).astype(BF16)

    chip = lax.div(u, 2)
    quarter = rows // 4

    def quarter_rows(group, near_chip):
        return pl.ds(pl.multiple_of((group * 2 + near_chip) * quarter, quarter), quarter)

    def send_mix(k):
        mine = quarter_rows(g, chip)
        remote(tm_hbm.at[mine], tm.at[s, mine], t_send, t_recv.at[0], at_place(1)).start()

    def mix_arrived(turn):
        drain(tm.at[pl.ds(0, seqs - 1), pl.ds(0, quarter)], t_recv.at[turn])

    def pass_mix():
        mix_arrived(0)
        part = tm.at[pl.ds(1 - odd, seqs - 1), quarter_rows(g, chip)]
        remote(part, part, t_send, t_recv.at[0], at_place(0)).start()

    def mix_share(k, near_chip, turn):
        for b in range(seqs):
            if b != k:
                part = tm.at[block_of(b), quarter_rows(g, near_chip)]
                device = (g, s, across) if turn == 1 else (1 - g, s, u)
                remote(part, part, f_send, t_recv.at[turn], device).start()

    def share_first(k):
        if k == 0:
            mix_arrived(0)
        mix_share(k, chip, 1)
        mix_share(k, chip, 2)

    def share_second(k):
        mix_arrived(1)
        mix_share(k, 1 - chip, 3)

    def mixed_copy(to, m):
        return remote(mixed_out.at[to], mixed_in.at[m], m_send, m_recv.at[m], at_place(to))

    def premix(c, k):
        last_row = pl.multiple_of(block_of(steps_of(c, k, COMPLETE)[-1][1]) * rows, rows)
        normed[pl.ds(last_row, rows)] = jnp.zeros((rows, inner), BF16)
        mix_arrived(2)
        mix_arrived(3)
        for b in range(seqs):
            first_row = pl.multiple_of(block_of(b) * rows, rows)
            mixed_sum[b] = normed[pl.ds(first_row, rows)].astype(F32) + dot(tm[block_of(b)], normed[...])

    def mix(c, k):
        last = steps_of(c, k, COMPLETE)[-1][1]
        last_rows = pl.ds(pl.multiple_of(block_of(last) * rows, rows), rows)
        late = normed[last_rows]
        for b in sorted(range(seqs), key=lambda b: -abs(b - k)):
            mixed = mixed_sum[b] + dot(tm[block_of(b), :, last_rows], late)
            if b == last:
                mixed = mixed + late.astype(F32)
            if b == k:
                mixed_in[k] = mixed.astype(BF16)
            else:
                mixed_out[b] = mixed.astype(BF16)
                mixed_copy(b, k).start()

    def act(c, k, step):
        kind, (m, b, to) = step // 1000, numbers_of(step)
        if kind == PASS:
            pass_queries(m, b, to)
        elif kind == ARRIVED:
            query_copy(m, b, k).wait_recv()
        elif kind == SEND_SUM:
            send_sum(c, k, m, b, to)
        elif kind == COMPLETE:
            sum_complete(c, k, m, b)
        elif kind == PIECE_ACROSS:
            across_arrived(step % 100)
        elif kind == PIECE_GROUP:
            group_arrived(step % 100)
        elif kind == SEND_MIX:
            send_mix(k)
        elif kind == PASS_MIX:
            pass_mix()
        elif kind == PREMIX:
            premix(c, k)
        elif kind == MIX:
            mix(c, k)
        elif kind == SHARE_FIRST:
            share_first(k)
        elif kind == SHARE_SECOND:
            share_second(k)

    def run(c, k, steps):
        for step in steps:
            act(c, k, step)

    parts = []
    for c, k in variants:
        parts.append([[]])
        skipped = early(c, k)
        for t in PLAN[c][k]:
            if t not in skipped:
                parts[-1][-1].append(t)
            if t // 1000 == ATTEND:
                parts[-1].append([])
    for index in range(users * seqs):
        by_variant(lambda c, k: run(c, k, parts[c * seqs + k][index][:-1]))
        chosen = [numbers_of(part[index][-1]) for part in parts]
        attend(pick([n[0] for n in chosen]), pick([n[1] for n in chosen]))
        if index == 0:
            pl.semaphore_wait(far, neighbours)
            loads["wg"].wait()
            loads["tm"].wait()
            for m in range(users):
                gates[m] = silu_of_double(dot(cand[user_of(m)], wg[...]) * 0.5)
    by_variant(lambda c, k: run(c, k, parts[c * seqs + k][-1]))

    loads["wo"].wait()
    slots = (u, partner, across, across_partner)
    for index in range(users):
        m = pick([TAIL_ORDER[c][k][index] for c, k in variants])

        @pl.when(place != m)
        def _():
            mixed_copy(place, m).wait_recv()

        user = user_of(m)
        gated = (mixed_in[m].astype(F32) * gates[m]).astype(BF16)
        state = cand[user].astype(F32) + dot(gated, wo[...])
        states[...] = state
        ffn_in = layer_norm(state).astype(BF16)
        if index == 0:
            loads["wu"].wait()
            remote(wu_hbm, wu.at[partner], w_send.at[0], wo_recv.at[0], (g, s, partner)).wait_recv()
            drain(wu.at[across_partner], wc_recv.at[0])
        hidden = [gelu_tanh(dot(ffn_in, wu[slot])).astype(BF16) for slot in slots]
        if index == 0:
            loads["wd"].wait()
            remote(wd_hbm, wd.at[partner], w_send.at[1], wo_recv.at[1], (g, s, partner)).wait_recv()
            drain(wd.at[across_partner], wc_recv.at[1])
        for start in range(0, width, COLUMNS):
            cols = slice(start, min(start + COLUMNS, width))
            total = states[:, cols]
            for h, slot in zip(hidden, slots):
                total = total + dot(h, wd[slot, :, cols])
            out_ref[user, :, cols] = total.astype(BF16)

    def finish(c, k):
        def blocks(kind):
            return incoming.at[pl.ds(0, len(steps_of(c, k, kind)))]

        drain(blocks(PASS), q_send)
        drain(blocks(SEND_SUM), p_send)
        drain(tm.at[pl.ds(0, seqs - 1 if k == 1 else 1), pl.ds(0, quarter)], t_send)
        if k < users:
            drain(tm.at[pl.ds(0, seqs - 1), pl.ds(0, 3 * quarter)], f_send)
            drain(incoming.at[pl.ds(0, seqs - 1)], m_send)

    by_variant(finish)
    drain(wu.at[pl.ds(0, 3)], w_send.at[0])
    drain(wd.at[pl.ds(0, 3)], w_send.at[1])


def fused(seqs, usrs, history_kv, candidates, lengths, w_query, w_gate, token_mix, w_out, w_up, w_down):
    users, hist, _ = history_kv.shape
    rows, width = candidates.shape[1:]
    inner = w_query.shape[1]
    depth = w_up.shape[1]
    dma = pltpu.SemaphoreType.DMA
    hbm = pl.BlockSpec(memory_space=pltpu.HBM)
    lanes = sum(lanes_of(m) for m in range(users))
    operands = (history_kv, candidates, lengths, w_query, w_gate, token_mix, w_out, w_up, w_down)
    return pl.pallas_call(
        functools.partial(kernel, seqs),
        out_shape=jax.ShapeDtypeStruct(candidates.shape, BF16),
        in_specs=[hbm] * len(operands),
        out_specs=pl.BlockSpec(memory_space=pltpu.VMEM),
        scratch_shapes=[
            pltpu.VMEM(history_kv.shape, BF16),
            pltpu.VMEM(candidates.shape, BF16),
            pltpu.VMEM(w_query.shape, BF16),
            pltpu.VMEM(w_gate.shape, BF16),
            pltpu.VMEM((seqs, *token_mix.shape), BF16),
            pltpu.VMEM(w_out.shape, BF16),
            pltpu.VMEM((usrs, width, depth), BF16),
            pltpu.VMEM((usrs, depth, width), BF16),
            pltpu.VMEM((users, hist, inner), BF16),
            pltpu.VMEM((users, seqs, rows, inner), BF16),
            pltpu.VMEM((users, seqs, rows, inner), F32),
            pltpu.VMEM((users, seqs, rows, inner), BF16),
            pltpu.VMEM((lanes * seqs, rows, inner), BF16),
            pltpu.VMEM((seqs * rows, inner), BF16),
            pltpu.VMEM((seqs, rows, inner), F32),
            pltpu.VMEM((seqs, rows, inner), BF16),
            pltpu.VMEM((users, rows, inner), BF16),
            pltpu.VMEM((users, rows, inner), F32),
            pltpu.VMEM((rows, width), F32),
            pltpu.SMEM(lengths.shape, jnp.int32),
            dma((9,)),
            dma, dma((users, seqs)), dma, dma((lanes, seqs)),
            dma, dma((4,)), dma, dma, dma((users,)),
            dma((2,)), dma((2,)), dma((2 * PIECES,)), dma((2 * PIECES,)), dma((2,)),
            pltpu.SemaphoreType.REGULAR,
        ],
        compiler_params=pltpu.CompilerParams(
            collective_id=0, has_side_effects=True, vmem_limit_bytes=34 * 1024 * 1024
        ),
        name="rank_layer",
    )(*(pltpu.with_memory_space_constraint(operand, pltpu.HBM) for operand in operands))


def shards(history_kv, candidates, lengths, w_query, w_gate, token_mix, w_out, w_up, w_down):
    user_count, hist_dev, _ = history_kv.shape
    inner = w_query.shape[1]
    half = hist_dev // 2
    scale = 1.0 / math.sqrt(DH)
    seq_index = lax.axis_index("seq")
    first_start = seq_index * hist_dev
    sections = ((history_kv[:, :half], first_start), (history_kv[:, half:], first_start + half))
    offsets = lax.iota(jnp.int32, half)
    queries = jnp.einsum(
        "ucd,de->uce", candidates, w_query, preferred_element_type=jnp.float32
    ).astype(jnp.bfloat16)
    piece = lax.all_gather(queries, "seq", axis=1, tiled=True)
    row_count = piece.shape[1]
    results = []
    for member in range(user_count):
        query_heads = piece[member].reshape(row_count, HEADS, DH)
        limit = lengths[member]
        summed = jnp.zeros((row_count, inner), jnp.float32)
        for section, section_start in sections:
            key_heads = section[member, :, :inner].reshape(half, HEADS, DH)
            value_heads = section[member, :, inner:].reshape(half, HEADS, DH)

            def compute(
                operand,
                key_heads=key_heads,
                value_heads=value_heads,
                section_start=section_start,
                query_heads=query_heads,
                limit=limit,
            ):
                scores = (
                    jnp.einsum(
                        "chd,thd->hct", query_heads, key_heads, preferred_element_type=jnp.float32
                    )
                    * scale
                )
                visible = section_start + offsets < limit
                weights = jnp.where(visible[None, None, :], jax.nn.silu(scores), 0.0).astype(
                    jnp.bfloat16
                )
                contrib = jnp.einsum(
                    "hct,thd->chd", weights, value_heads, preferred_element_type=jnp.float32
                )
                return contrib.reshape(row_count, inner)

            def skipped(operand):
                return jnp.zeros((row_count, inner), jnp.float32)

            summed = summed + lax.cond(section_start < limit, compute, skipped, 0)
        results.append(summed)
    partial_sums = jnp.stack(results)
    attended = lax.psum_scatter(partial_sums, "seq", scatter_dimension=1, tiled=True)
    normed = layer_norm(attended).astype(jnp.bfloat16)
    mixed = normed.astype(jnp.float32) + jnp.einsum(
        "cp,upe->uce",
        token_mix,
        lax.all_gather(normed, "seq", axis=1, tiled=True),
        preferred_element_type=jnp.float32,
    )
    gate_values = jax.nn.silu(
        jnp.einsum("ucd,de->uce", candidates, w_gate, preferred_element_type=jnp.float32)
    )
    gated = (mixed * gate_values).astype(jnp.bfloat16)
    state = candidates.astype(jnp.float32) + jnp.einsum(
        "uce,ed->ucd", gated, w_out, preferred_element_type=jnp.float32
    )
    ffn_in = layer_norm(state).astype(jnp.bfloat16)
    hidden = jax.nn.gelu(
        jnp.einsum(
            "ucd,df->ucf",
            lax.all_gather(ffn_in, "usr", axis=0, tiled=True),
            w_up,
            preferred_element_type=jnp.float32,
        )
    ).astype(jnp.bfloat16)
    ffn_terms = jnp.einsum("ucf,fd->ucd", hidden, w_down, preferred_element_type=jnp.float32)
    ffn_out = lax.psum_scatter(
        ffn_terms.astype(jnp.bfloat16), "usr", scatter_dimension=0, tiled=True
    ).astype(jnp.float32)
    return (state + ffn_out).astype(jnp.bfloat16)


def solution(mesh):
    sizes = dict(mesh.shape)
    seqs, usrs = sizes["seq"], sizes["usr"]
    def body(history_kv, candidates, *rest):
        operands = (history_kv, candidates, *rest)
        fits = sizes["grp"] == 2 and usrs == 4 and seqs == len(PLAN[0])
        if fits and candidates.shape[0] == len(QUERY_ORDER[0][0]):
            return fused(seqs, usrs, *operands)
        return shards(*operands)

    return jax.shard_map(
        body,
        mesh=mesh,
        in_specs=(
            P(("grp", "usr"), "seq", None),
            P(("grp", "usr"), "seq", None),
            P(("grp", "usr")),
            P(),
            P(),
            P("seq", None),
            P(),
            P(None, "usr"),
            P("usr", None),
        ),
        out_specs=P(("grp", "usr"), "seq", None),
        check_vma=False,
    )
```

```python
import functools
import math

import jax
import jax.numpy as jnp
from jax import lax
from jax.experimental import pallas as pl
from jax.experimental.pallas import tpu as pltpu
from jax.sharding import PartitionSpec as P

HEADS = 3
DH = 128
F32 = jnp.float32
BF16 = jnp.bfloat16
MESH = pl.DeviceIdType.MESH
COLUMNS = 256
PIECES = 4
DEPTH = 4
LATE_LOADS = 6

(ATTEND, ARRIVED, PASS, SEND_SUM, COMPLETE, PIECE_ACROSS, PIECE_GROUP, SEND_MIX, PASS_MIX, PREMIX, MIX,
 SHARE_FIRST, SHARE_SECOND) = range(1, 14)
PLAN = (
    (
        (
            3101, 3001, 1000, 8000, 1100, 4101, 6000, 2010, 1010, 6001, 2110, 1110, 4111, 2020, 7000,
            1020, 6002, 12000, 7001, 6003, 2120, 1120, 4121, 6004, 7002, 2130, 1130, 4131, 13000, 7003,
            6005, 5020, 7004, 6006, 2030, 1030, 6007, 5030, 5010, 10000, 5000, 11000, 7005, 7006, 7007,
        ),
        (
            3012, 1010, 3010, 1110, 3110, 3112, 2020, 3020, 1020, 2100, 4020, 1100, 2000, 3002, 6000,
            3102, 1000, 4000, 2120, 1120, 9000, 12000, 6001, 3120, 2130, 3130, 1130, 6002, 7000, 13000,
            6003, 7001, 6004, 2030, 7002, 3030, 1030, 4030, 5120, 6005, 4010, 5130, 6006, 7003, 5110,
            6007, 10000, 5100, 11000, 7004, 7005, 7006, 7007,
        ),
        (
            3021, 3121, 3123, 1020, 8000, 1120, 4121, 2010, 1010, 3013, 6000, 2130, 3131, 1130, 3023,
            6001, 4131, 2110, 3113, 1110, 6002, 7000, 2000, 1000, 3003, 2100, 3103, 1100, 6003, 4101,
            7001, 2030, 3031, 1030, 4031, 6004, 7002, 4011, 4020, 6005, 7003, 4111, 6006, 7004, 4000,
            6007, 7005, 7006, 7007,
        ),
        (
            3132, 1130, 8000, 4132, 1030, 4032, 3032, 6000, 2120, 1120, 4121, 6001, 7000, 6002, 2010,
            1010, 4012, 7001, 2020, 1020, 4022, 6003, 7002, 2110, 1110, 4112, 6004, 2000, 1000, 4002,
            7003, 6005, 2100, 1100, 4101, 7004, 6006, 7005, 6007, 7006, 7007,
        ),
    ),
    (
        (
            3101, 1000, 8000, 1100, 4101, 3001, 6000, 2010, 1010, 6001, 2020, 1020, 7000, 6002, 7001,
            12000, 6003, 7002, 2110, 1110, 4111, 6004, 13000, 2120, 1120, 4121, 7003, 6005, 2130, 1130,
            4131, 7004, 6006, 2030, 1030, 5030, 6007, 5020, 7005, 5000, 10000, 5010, 11000, 7006, 7007,
        ),
        (
            3112, 1010, 4010, 1110, 3010, 2020, 3020, 1020, 6000, 2100, 1100, 3102, 3012, 6001, 9000,
            12000, 3110, 6002, 7000, 2000, 3002, 1000, 6003, 7001, 2120, 3120, 1120, 2130, 3130, 1130,
            13000, 6004, 7002, 2030, 3030, 1030, 6005, 7003, 4030, 4020, 6006, 4000, 5120, 5110, 6007,
            7004, 5100, 10000, 5130, 11000, 7005, 7006, 7007,
        ),
        (
            3023, 3123, 3021, 1120, 4121, 8000, 1020, 2110, 1110, 6000, 6001, 6002, 7000, 3121, 3113,
            2130, 3131, 1130, 4131, 2100, 3103, 1100, 6003, 7001, 2030, 3031, 1030, 4031, 2010, 3013,
            1010, 6004, 7002, 4021, 2000, 3003, 1000, 4001, 6005, 7003, 4111, 6006, 7004, 4101, 6007,
            7005, 4010, 7006, 7007,
        ),
        (
            1030, 8000, 1130, 4132, 3132, 4032, 2020, 1020, 3032, 4022, 2120, 1120, 4121, 6000, 6001,
            7000, 6002, 7001, 6003, 2110, 1110, 4112, 6004, 7002, 2100, 1100, 6005, 4102, 7003, 2010,
            1010, 6006, 4012, 7004, 2000, 1000, 4000, 7005, 6007, 7006, 7007,
        ),
    ),
)
QUERY_ORDER = (((0, 1), (0, 1), (0, 1), (0, 1)), ((0, 1), (0, 1), (0, 1), (0, 1)))
TAIL_ORDER = (((0, 1), (1, 0), (0, 1), (1, 0)), ((0, 1), (1, 0), (0, 1), (1, 0)))


def numbers_of(step):
    return step // 100 % 10, step // 10 % 10, step % 10


def steps_of(odd, k, kind):
    return [numbers_of(t) for t in PLAN[odd][k] if t // 1000 == kind]


def children(odd, k, m, b):
    return [j for j in range(len(PLAN[odd])) if (m, b, k) in steps_of(odd, j, SEND_SUM)]


def lanes_of(m):
    places = range(len(PLAN[0]))
    return max(len(children(odd, k, m, b)) for odd in range(2) for k in places for b in places)


def layer_norm(values):
    center = values - jnp.mean(values, axis=-1, keepdims=True)
    spread = jnp.mean(center * center, axis=-1, keepdims=True)
    return center * lax.rsqrt(spread + 1e-05)


def silu_of_double(half):
    return half + half * jnp.tanh(half)


def gelu_tanh(v):
    slope = math.sqrt(2.0 / math.pi)
    half = 0.5 * v
    return half + half * jnp.tanh(v * (slope + (0.044715 * slope) * (v * v)))


def dot(a, b):
    return jnp.dot(a, b, preferred_element_type=F32)


def kernel(
    seqs,
    kv_hbm, cand_hbm, len_hbm, wq_hbm, wg_hbm, tm_hbm, wo_hbm, wu_hbm, wd_hbm,
    out_ref,
    kv, cand, wq, wg, tm, wo, wu, wd,
    values, queries, sums, outgoing, incoming, normed, mixed_sum, mixed_out, mixed_in, gates, states,
    lens, load_sem,
    q_send, q_recv, p_send, p_recv, t_send, t_recv, f_send, m_send, m_recv,
    w_send, wo_recv, wx_recv, wy_recv, wc_recv, far,
):
    users, rows, width = cand.shape
    hist = kv.shape[1]
    inner = wq.shape[1]
    g, s, u = lax.axis_index("grp"), lax.axis_index("seq"), lax.axis_index("usr")
    odd = lax.rem(u, 2)
    partner = u + 1 - 2 * odd
    across = lax.rem(u + 2, 4)
    across_partner = lax.rem(partner + 2, 4)
    step = 1 - 2 * odd
    place = s + odd * (seqs - 1 - 2 * s)

    def user_of(m):
        return m + odd * (users - 1 - 2 * m)

    def block_of(b):
        return b + odd * (seqs - 1 - 2 * b)

    def at_place(b):
        return (g, block_of(b), u)

    variants = [(c, k) for c in range(2) for k in range(seqs)]
    variant = odd * seqs + place

    def pick(choices):
        if len(set(choices)) == 1:
            return choices[0]
        value = choices[-1]
        for v in range(len(choices) - 1):
            value = jnp.where(variant == v, choices[v], value)
        return value

    def by_variant(do):
        for v, (c, k) in enumerate(variants):
            @pl.when(variant == v)
            def _():
                do(c, k)

    loads = {}
    for index, (name, source, target) in enumerate((
        ("cand", cand_hbm, cand), ("wq", wq_hbm, wq), ("lens", len_hbm, lens), ("kv", kv_hbm, kv), ("wg", wg_hbm, wg),
        ("tm", tm_hbm, tm.at[s]), ("wo", wo_hbm, wo), ("wu", wu_hbm, wu.at[u]), ("wd", wd_hbm, wd.at[u]),
    )):
        loads[name] = pltpu.make_async_copy(source, target, load_sem.at[index])

    for name in ("cand", "wq", "lens"):
        loads[name].start()

    barrier = pltpu.get_barrier_semaphore()
    near = [(g, s, partner), (g, s, across), (1 - g, s, u)]
    for peer in near:
        pl.semaphore_signal(barrier, inc=1, device_id=peer, device_id_type=MESH)

    @pl.when(s > 0)
    def _():
        pl.semaphore_signal(barrier, inc=1, device_id=(g, s - 1, u), device_id_type=MESH)

    @pl.when(s < seqs - 1)
    def _():
        pl.semaphore_signal(barrier, inc=1, device_id=(g, s + 1, u), device_id_type=MESH)

    def remote(source, target, send, recv, device):
        return pltpu.make_async_remote_copy(
            src_ref=source, dst_ref=target, send_sem=send, recv_sem=recv,
            device_id=device, device_id_type=MESH,
        )

    def drain(ref, sem):
        pltpu.make_async_copy(ref, ref, sem).wait()

    weights = ((wu_hbm, wu), (wd_hbm, wd))

    def rows_of(piece, half):
        size = weights[piece // PIECES][1].shape[1] // (2 * PIECES)
        return pl.ds(pl.multiple_of((half * PIECES + piece % PIECES) * size, size), size)

    def piece_of(piece, slot, half):
        return weights[piece // PIECES][1].at[slot, rows_of(piece, half)]

    def to_partner_own(w):
        return remote(weights[w][0], weights[w][1].at[u], w_send.at[w], wo_recv.at[w], (g, s, partner))

    def to_across(piece, slot):
        w = piece // PIECES
        source = weights[w][0].at[rows_of(piece, g)]
        return remote(source, piece_of(piece, slot, g), w_send.at[w], wx_recv.at[piece], (g, s, across))

    def to_group(piece, half):
        part = piece_of(piece, across, half)
        return remote(part, part, w_send.at[piece // PIECES], wy_recv.at[piece], (1 - g, s, u))

    def to_partner_far(piece, half):
        part = piece_of(piece, across, half)
        w = piece // PIECES
        return remote(part, part, w_send.at[w], wc_recv.at[w], (g, s, partner))

    def across_arrived(piece):
        to_across(piece, across).wait_recv()
        if piece + DEPTH < 2 * PIECES:
            to_across(piece + DEPTH, u).start()
        to_group(piece, g).start()
        to_partner_far(piece, g).start()

    def group_arrived(piece):
        to_group(piece, 1 - g).wait_recv()
        to_partner_far(piece, 1 - g).start()

    def query_copy(m, b, to):
        ref = queries.at[m, b]
        return remote(ref, ref, q_send, q_recv.at[m, b], at_place(to))

    def early(c, k):
        kinds = [t // 1000 for t in PLAN[c][k]]
        ahead = [t for t in PLAN[c][k][:kinds.index(ATTEND)] if t // 1000 == PASS]
        return [t for t in ahead if numbers_of(t)[:2] == (QUERY_ORDER[c][k][0], k) and abs(t % 10 - k) == 1]

    def pass_queries(m, b, to):
        query_copy(m, b, to).start()

    def send_early(c, k):
        for t in early(c, k):
            pass_queries(*numbers_of(t))

    orders = [QUERY_ORDER[c][k] for c, k in variants]
    first, second = pick([o[0] for o in orders]), pick([o[1] for o in orders])
    loads["cand"].wait()
    loads["wq"].wait()
    loads["kv"].start()
    queries[first, place] = dot(cand[user_of(first)], wq[...]).astype(BF16)
    neighbours = (s > 0).astype(jnp.int32) + (s < seqs - 1).astype(jnp.int32)
    pl.semaphore_wait(barrier, len(near) + neighbours)
    by_variant(send_early)
    for piece in range(DEPTH):
        to_across(piece, u).start()
    for way in (-1, 1):
        @pl.when((s + way >= 0) & (s + way < seqs))
        def _():
            pl.semaphore_signal(far, inc=1, device_id=(g, s + way, u), device_id_type=MESH)

    queries[second, place] = dot(cand[user_of(second)], wq[...]).astype(BF16)
    for name in ("wg", "tm"):
        loads[name].start()

    half_scale = 0.5 / math.sqrt(DH)

    def attend(m, b):
        user = user_of(m)
        for head in range(HEADS):
            cols = slice(head * DH, (head + 1) * DH)
            scores = lax.dot_general(
                queries[m, b, :, cols], kv[user, :, cols], (((1,), (1,)), ((), ())),
                preferred_element_type=F32,
            )
            weight = silu_of_double(scores * half_scale).astype(BF16)
            sums[m, b, :, cols] = dot(weight, values[user, :, cols])

    lane_start = [sum(lanes_of(j) for j in range(m)) for m in range(users)]

    def sum_copy(c, source, m, b, to):
        lane = lane_start[m] + children(c, to, m, b).index(source)
        return remote(
            outgoing.at[m, b], incoming.at[lane * seqs + b], p_send, p_recv.at[lane, b], at_place(to)
        )

    def gather_sum(c, k, m, b):
        total = sums[m, b]
        for child in children(c, k, m, b):
            copy = sum_copy(c, child, m, b, k)
            copy.wait_recv()
            lane = lane_start[m] + children(c, k, m, b).index(child)
            total = total + incoming[lane * seqs + b].astype(F32)
        return total

    def send_sum(c, k, m, b, to):
        outgoing[m, b] = gather_sum(c, k, m, b).astype(BF16)
        sum_copy(c, k, m, b, to).start()

    def sum_complete(c, k, m, b):
        first_row = pl.multiple_of(block_of(b) * rows, rows)
        normed[pl.ds(first_row, rows)] = layer_norm(gather_sum(c, k, m, b)).astype(BF16)

    chip = lax.div(u, 2)
    quarter = rows // 4

    def quarter_rows(group, near_chip):
        return pl.ds(pl.multiple_of((group * 2 + near_chip) * quarter, quarter), quarter)

    def send_mix(k):
        mine = quarter_rows(g, chip)
        remote(tm_hbm.at[mine], tm.at[s, mine], t_send, t_recv.at[0], at_place(1)).start()

    def mix_arrived(turn):
        drain(tm.at[pl.ds(0, seqs - 1), pl.ds(0, quarter)], t_recv.at[turn])

    def pass_mix():
        mix_arrived(0)
        part = tm.at[pl.ds(1 - odd, seqs - 1), quarter_rows(g, chip)]
        remote(part, part, t_send, t_recv.at[0], at_place(0)).start()

    def mix_share(k, near_chip, turn):
        for b in range(seqs):
            if b != k:
                part = tm.at[block_of(b), quarter_rows(g, near_chip)]
                device = (g, s, across) if turn == 1 else (1 - g, s, u)
                remote(part, part, f_send, t_recv.at[turn], device).start()

    def share_first(k):
        if k == 0:
            mix_arrived(0)
        mix_share(k, chip, 1)
        mix_share(k, chip, 2)

    def share_second(k):
        mix_arrived(1)
        mix_share(k, 1 - chip, 3)

    def mixed_copy(to, m):
        return remote(mixed_out.at[to], mixed_in.at[m], m_send, m_recv.at[m], at_place(to))

    def premix(c, k):
        last_row = pl.multiple_of(block_of(steps_of(c, k, COMPLETE)[-1][1]) * rows, rows)
        normed[pl.ds(last_row, rows)] = jnp.zeros((rows, inner), BF16)
        mix_arrived(2)
        mix_arrived(3)
        for b in range(seqs):
            first_row = pl.multiple_of(block_of(b) * rows, rows)
            mixed_sum[b] = normed[pl.ds(first_row, rows)].astype(F32) + dot(tm[block_of(b)], normed[...])

    def mix(c, k):
        last = steps_of(c, k, COMPLETE)[-1][1]
        last_rows = pl.ds(pl.multiple_of(block_of(last) * rows, rows), rows)
        late = normed[last_rows]
        for b in sorted(range(seqs), key=lambda b: -abs(b - k)):
            mixed = mixed_sum[b] + dot(tm[block_of(b), :, last_rows], late)
            if b == last:
                mixed = mixed + late.astype(F32)
            if b == k:
                mixed_in[k] = mixed.astype(BF16)
            else:
                mixed_out[b] = mixed.astype(BF16)
                mixed_copy(b, k).start()

    def act(c, k, step):
        kind, (m, b, to) = step // 1000, numbers_of(step)
        if kind == PASS:
            pass_queries(m, b, to)
        elif kind == ARRIVED:
            query_copy(m, b, k).wait_recv()
        elif kind == SEND_SUM:
            send_sum(c, k, m, b, to)
        elif kind == COMPLETE:
            sum_complete(c, k, m, b)
        elif kind == PIECE_ACROSS:
            across_arrived(step % 100)
        elif kind == PIECE_GROUP:
            group_arrived(step % 100)
        elif kind == SEND_MIX:
            send_mix(k)
        elif kind == PASS_MIX:
            pass_mix()
        elif kind == PREMIX:
            premix(c, k)
        elif kind == MIX:
            mix(c, k)
        elif kind == SHARE_FIRST:
            share_first(k)
        elif kind == SHARE_SECOND:
            share_second(k)

    def run(c, k, steps):
        for step in steps:
            act(c, k, step)

    parts = []
    for c, k in variants:
        parts.append([[]])
        skipped = early(c, k)
        for t in PLAN[c][k]:
            if t not in skipped:
                parts[-1][-1].append(t)
            if t // 1000 == ATTEND:
                parts[-1].append([])
    for index in range(users * seqs):
        by_variant(lambda c, k: run(c, k, parts[c * seqs + k][index][:-1]))
        if index == 0:
            loads["lens"].wait()
            loads["kv"].wait()
            for m in range(users):
                slots = s * hist + lax.broadcasted_iota(jnp.int32, (hist, 1), 0)
                visible = jnp.where(slots < lens[m], 1.0, 0.0)
                values[m] = (kv[m, :, inner:].astype(F32) * visible).astype(BF16)
        chosen = [numbers_of(part[index][-1]) for part in parts]
        attend(pick([n[0] for n in chosen]), pick([n[1] for n in chosen]))
        if index == 0:
            pl.semaphore_wait(far, neighbours)
            loads["wg"].wait()
            loads["tm"].wait()
            for m in range(users):
                gates[m] = silu_of_double(dot(cand[user_of(m)], wg[...]) * 0.5)
        if index == LATE_LOADS:
            for w in range(2):
                to_partner_own(w).start()
            for name in ("wo", "wu", "wd"):
                loads[name].start()
    by_variant(lambda c, k: run(c, k, parts[c * seqs + k][-1]))

    loads["wo"].wait()
    slots = (u, partner, across, across_partner)
    for index in range(users):
        m = pick([TAIL_ORDER[c][k][index] for c, k in variants])

        @pl.when(place != m)
        def _():
            mixed_copy(place, m).wait_recv()

        user = user_of(m)
        gated = (mixed_in[m].astype(F32) * gates[m]).astype(BF16)
        state = cand[user].astype(F32) + dot(gated, wo[...])
        states[...] = state
        ffn_in = layer_norm(state).astype(BF16)
        if index == 0:
            loads["wu"].wait()
            remote(wu_hbm, wu.at[partner], w_send.at[0], wo_recv.at[0], (g, s, partner)).wait_recv()
            drain(wu.at[across_partner], wc_recv.at[0])
        hidden = [gelu_tanh(dot(ffn_in, wu[slot])).astype(BF16) for slot in slots]
        if index == 0:
            loads["wd"].wait()
            remote(wd_hbm, wd.at[partner], w_send.at[1], wo_recv.at[1], (g, s, partner)).wait_recv()
            drain(wd.at[across_partner], wc_recv.at[1])
        for start in range(0, width, COLUMNS):
            cols = slice(start, min(start + COLUMNS, width))
            total = states[:, cols]
            for h, slot in zip(hidden, slots):
                total = total + dot(h, wd[slot, :, cols])
            out_ref[user, :, cols] = total.astype(BF16)

    def finish(c, k):
        def blocks(kind):
            return incoming.at[pl.ds(0, len(steps_of(c, k, kind)))]

        drain(blocks(PASS), q_send)
        drain(blocks(SEND_SUM), p_send)
        drain(tm.at[pl.ds(0, seqs - 1 if k == 1 else 1), pl.ds(0, quarter)], t_send)
        if k < users:
            drain(tm.at[pl.ds(0, seqs - 1), pl.ds(0, 3 * quarter)], f_send)
            drain(incoming.at[pl.ds(0, seqs - 1)], m_send)

    by_variant(finish)
    drain(wu.at[pl.ds(0, 3)], w_send.at[0])
    drain(wd.at[pl.ds(0, 3)], w_send.at[1])


def fused(seqs, usrs, history_kv, candidates, lengths, w_query, w_gate, token_mix, w_out, w_up, w_down):
    users, hist, _ = history_kv.shape
    rows, width = candidates.shape[1:]
    inner = w_query.shape[1]
    depth = w_up.shape[1]
    dma = pltpu.SemaphoreType.DMA
    hbm = pl.BlockSpec(memory_space=pltpu.HBM)
    lanes = sum(lanes_of(m) for m in range(users))
    operands = (history_kv, candidates, lengths, w_query, w_gate, token_mix, w_out, w_up, w_down)
    return pl.pallas_call(
        functools.partial(kernel, seqs),
        out_shape=jax.ShapeDtypeStruct(candidates.shape, BF16),
        in_specs=[hbm] * len(operands),
        out_specs=pl.BlockSpec(memory_space=pltpu.VMEM),
        scratch_shapes=[
            pltpu.VMEM(history_kv.shape, BF16),
            pltpu.VMEM(candidates.shape, BF16),
            pltpu.VMEM(w_query.shape, BF16),
            pltpu.VMEM(w_gate.shape, BF16),
            pltpu.VMEM((seqs, *token_mix.shape), BF16),
            pltpu.VMEM(w_out.shape, BF16),
            pltpu.VMEM((usrs, width, depth), BF16),
            pltpu.VMEM((usrs, depth, width), BF16),
            pltpu.VMEM((users, hist, inner), BF16),
            pltpu.VMEM((users, seqs, rows, inner), BF16),
            pltpu.VMEM((users, seqs, rows, inner), F32),
            pltpu.VMEM((users, seqs, rows, inner), BF16),
            pltpu.VMEM((lanes * seqs, rows, inner), BF16),
            pltpu.VMEM((seqs * rows, inner), BF16),
            pltpu.VMEM((seqs, rows, inner), F32),
            pltpu.VMEM((seqs, rows, inner), BF16),
            pltpu.VMEM((users, rows, inner), BF16),
            pltpu.VMEM((users, rows, inner), F32),
            pltpu.VMEM((rows, width), F32),
            pltpu.SMEM(lengths.shape, jnp.int32),
            dma((9,)),
            dma, dma((users, seqs)), dma, dma((lanes, seqs)),
            dma, dma((4,)), dma, dma, dma((users,)),
            dma((2,)), dma((2,)), dma((2 * PIECES,)), dma((2 * PIECES,)), dma((2,)),
            pltpu.SemaphoreType.REGULAR,
        ],
        compiler_params=pltpu.CompilerParams(
            collective_id=0, has_side_effects=True, vmem_limit_bytes=34 * 1024 * 1024
        ),
        name="rank_layer",
    )(*(pltpu.with_memory_space_constraint(operand, pltpu.HBM) for operand in operands))


def shards(history_kv, candidates, lengths, w_query, w_gate, token_mix, w_out, w_up, w_down):
    user_count, hist_dev, _ = history_kv.shape
    inner = w_query.shape[1]
    half = hist_dev // 2
    scale = 1.0 / math.sqrt(DH)
    seq_index = lax.axis_index("seq")
    first_start = seq_index * hist_dev
    sections = ((history_kv[:, :half], first_start), (history_kv[:, half:], first_start + half))
    offsets = lax.iota(jnp.int32, half)
    queries = jnp.einsum(
        "ucd,de->uce", candidates, w_query, preferred_element_type=jnp.float32
    ).astype(jnp.bfloat16)
    piece = lax.all_gather(queries, "seq", axis=1, tiled=True)
    row_count = piece.shape[1]
    results = []
    for member in range(user_count):
        query_heads = piece[member].reshape(row_count, HEADS, DH)
        limit = lengths[member]
        summed = jnp.zeros((row_count, inner), jnp.float32)
        for section, section_start in sections:
            key_heads = section[member, :, :inner].reshape(half, HEADS, DH)
            value_heads = section[member, :, inner:].reshape(half, HEADS, DH)

            def compute(
                operand,
                key_heads=key_heads,
                value_heads=value_heads,
                section_start=section_start,
                query_heads=query_heads,
                limit=limit,
            ):
                scores = (
                    jnp.einsum(
                        "chd,thd->hct", query_heads, key_heads, preferred_element_type=jnp.float32
                    )
                    * scale
                )
                visible = section_start + offsets < limit
                weights = jnp.where(visible[None, None, :], jax.nn.silu(scores), 0.0).astype(
                    jnp.bfloat16
                )
                contrib = jnp.einsum(
                    "hct,thd->chd", weights, value_heads, preferred_element_type=jnp.float32
                )
                return contrib.reshape(row_count, inner)

            def skipped(operand):
                return jnp.zeros((row_count, inner), jnp.float32)

            summed = summed + lax.cond(section_start < limit, compute, skipped, 0)
        results.append(summed)
    partial_sums = jnp.stack(results)
    attended = lax.psum_scatter(partial_sums, "seq", scatter_dimension=1, tiled=True)
    normed = layer_norm(attended).astype(jnp.bfloat16)
    mixed = normed.astype(jnp.float32) + jnp.einsum(
        "cp,upe->uce",
        token_mix,
        lax.all_gather(normed, "seq", axis=1, tiled=True),
        preferred_element_type=jnp.float32,
    )
    gate_values = jax.nn.silu(
        jnp.einsum("ucd,de->uce", candidates, w_gate, preferred_element_type=jnp.float32)
    )
    gated = (mixed * gate_values).astype(jnp.bfloat16)
    state = candidates.astype(jnp.float32) + jnp.einsum(
        "uce,ed->ucd", gated, w_out, preferred_element_type=jnp.float32
    )
    ffn_in = layer_norm(state).astype(jnp.bfloat16)
    hidden = jax.nn.gelu(
        jnp.einsum(
            "ucd,df->ucf",
            lax.all_gather(ffn_in, "usr", axis=0, tiled=True),
            w_up,
            preferred_element_type=jnp.float32,
        )
    ).astype(jnp.bfloat16)
    ffn_terms = jnp.einsum("ucf,fd->ucd", hidden, w_down, preferred_element_type=jnp.float32)
    ffn_out = lax.psum_scatter(
        ffn_terms.astype(jnp.bfloat16), "usr", scatter_dimension=0, tiled=True
    ).astype(jnp.float32)
    return (state + ffn_out).astype(jnp.bfloat16)


def solution(mesh):
    sizes = dict(mesh.shape)
    seqs, usrs = sizes["seq"], sizes["usr"]
    def body(history_kv, candidates, *rest):
        operands = (history_kv, candidates, *rest)
        fits = sizes["grp"] == 2 and usrs == 4 and seqs == len(PLAN[0])
        if fits and candidates.shape[0] == len(QUERY_ORDER[0][0]):
            return fused(seqs, usrs, *operands)
        return shards(*operands)

    return jax.shard_map(
        body,
        mesh=mesh,
        in_specs=(
            P(("grp", "usr"), "seq", None),
            P(("grp", "usr"), "seq", None),
            P(("grp", "usr")),
            P(),
            P(),
            P("seq", None),
            P(),
            P(None, "usr"),
            P("usr", None),
        ),
        out_specs=P(("grp", "usr"), "seq", None),
        check_vma=False,
    )
```

```python
import functools
import math

import jax
import jax.numpy as jnp
from jax import lax
from jax.experimental import pallas as pl
from jax.experimental.pallas import tpu as pltpu
from jax.sharding import PartitionSpec as P

HEADS = 3
DH = 128
F32 = jnp.float32
BF16 = jnp.bfloat16
MESH = pl.DeviceIdType.MESH
COLUMNS = 256
PIECES = 4
DEPTH = 3
LATE_LOADS = 6

(ATTEND, ARRIVED, PASS, SEND_SUM, COMPLETE, PIECE_ACROSS, PIECE_GROUP, SEND_MIX, PASS_MIX, PREMIX, MIX,
 SHARE_FIRST, SHARE_SECOND) = range(1, 14)
PLAN = (
    (
        (
            3001, 3101, 1100, 4101, 8000, 1000, 2010, 1010, 6000, 2110, 1110, 4111, 6001, 6002, 7000,
            6003, 7001, 12000, 6004, 7002, 2130, 1130, 6005, 4131, 7003, 2020, 1020, 2120, 1120, 4121,
            13000, 5020, 6006, 7004, 2030, 1030, 5030, 6007, 7005, 5000, 10000, 5010, 11000, 7006, 7007,
        ),
        (
            3010, 3012, 3110, 3112, 1110, 1010, 2000, 3002, 1000, 4000, 6000, 2100, 3102, 1100, 6001,
            9000, 12000, 6002, 7000, 2130, 3130, 1130, 6003, 7001, 2020, 3020, 1020, 2120, 3120, 1120,
            13000, 4020, 6004, 7002, 2030, 3030, 1030, 4030, 6005, 7003, 4010, 6006, 5130, 5110, 6007,
            7004, 5120, 10000, 5100, 11000, 7005, 7006, 7007,
        ),
        (
            3123, 3023, 1120, 8000, 1020, 4021, 2010, 3013, 1010, 6000, 2130, 1130, 3131, 2110, 3113,
            1110, 3021, 3121, 6001, 4131, 6002, 7000, 2000, 3003, 1000, 2100, 3103, 1100, 6003, 7001,
            2030, 3031, 1030, 4031, 6004, 7002, 4121, 6005, 7003, 4011, 4111, 6006, 7004, 4000, 4101,
            6007, 7005, 7006, 7007,
        ),
        (
            3132, 1030, 8000, 1130, 4132, 4032, 2120, 1120, 3032, 4122, 6000, 2020, 1020, 4021, 6001,
            2010, 1010, 4012, 7000, 6002, 2110, 1110, 6003, 7001, 4112, 2000, 1000, 4002, 7002, 6004,
            2100, 1100, 4102, 7003, 6005, 7004, 6006, 7005, 6007, 7006, 7007,
        ),
    ),
    (
        (
            3001, 3101, 1000, 8000, 1100, 4101, 6000, 2110, 1110, 6001, 4111, 7000, 6002, 12000, 6003,
            7001, 7002, 6004, 13000, 2010, 1010, 2130, 1130, 4131, 7003, 6005, 2120, 1120, 4121, 2020,
            1020, 7004, 6006, 5020, 2030, 1030, 6007, 5030, 5010, 7005, 10000, 5000, 11000, 7006, 7007,
        ),
        (
            3112, 3012, 1010, 4010, 1110, 3110, 2000, 3002, 1000, 6000, 4000, 2120, 1120, 2100, 3102,
            1100, 6001, 9000, 12000, 6002, 7000, 2130, 1130, 3010, 3130, 3120, 6003, 7001, 2020, 3020,
            1020, 13000, 6004, 7002, 4020, 2030, 3030, 1030, 6005, 7003, 4030, 5100, 5130, 6006, 5110,
            10000, 5120, 11000, 6007, 7004, 7005, 7006, 7007,
        ),
        (
            3023, 3121, 1020, 8000, 1120, 4121, 3123, 2110, 3113, 1110, 2010, 3013, 1010, 6000, 6001,
            2130, 3131, 1130, 2000, 3003, 3021, 1000, 4131, 6002, 7000, 2100, 3103, 1100, 4101, 6003,
            7001, 4021, 2030, 3031, 1030, 4031, 7002, 6004, 4111, 6005, 7003, 4010, 4000, 6006, 7004,
            6007, 7005, 7006, 7007,
        ),
        (
            1130, 8000, 3132, 4132, 1030, 4032, 2020, 1020, 6000, 4022, 3032, 2120, 1120, 4121, 6001,
            2110, 1110, 4112, 6002, 7000, 2010, 1010, 4012, 2000, 1000, 6003, 7001, 4002, 2100, 1100,
            7002, 6004, 4101, 6005, 7003, 6006, 7004, 6007, 7005, 7006, 7007,
        ),
    ),
)
QUERY_ORDER = (((0, 1), (0, 1), (0, 1), (0, 1)), ((0, 1), (0, 1), (0, 1), (0, 1)))
TAIL_ORDER = (((0, 1), (1, 0), (0, 1), (1, 0)), ((0, 1), (1, 0), (0, 1), (1, 0)))


def numbers_of(step):
    return step // 100 % 10, step // 10 % 10, step % 10


def steps_of(odd, k, kind):
    return [numbers_of(t) for t in PLAN[odd][k] if t // 1000 == kind]


def children(odd, k, m, b):
    return [j for j in range(len(PLAN[odd])) if (m, b, k) in steps_of(odd, j, SEND_SUM)]


def lanes_of(m):
    places = range(len(PLAN[0]))
    return max(len(children(odd, k, m, b)) for odd in range(2) for k in places for b in places)


def layer_norm(values):
    center = values - jnp.mean(values, axis=-1, keepdims=True)
    spread = jnp.mean(center * center, axis=-1, keepdims=True)
    return center * lax.rsqrt(spread + 1e-05)


def silu_of_double(half):
    return half + half * jnp.tanh(half)


def gelu_tanh(v):
    slope = math.sqrt(2.0 / math.pi)
    half = 0.5 * v
    return half + half * jnp.tanh(v * (slope + (0.044715 * slope) * (v * v)))


def dot(a, b):
    return jnp.dot(a, b, preferred_element_type=F32)


def kernel(
    seqs,
    kv_hbm, cand_hbm, len_hbm, wq_hbm, wg_hbm, tm_hbm, wo_hbm, wu_hbm, wd_hbm,
    out_ref,
    kv, cand, wq, wg, tm, wo, wu, wd,
    values, queries, sums, outgoing, incoming, normed, mixed_sum, mixed_out, mixed_in, gates, states,
    lens, load_sem,
    q_send, q_recv, p_send, p_recv, t_send, t_recv, f_send, m_send, m_recv,
    w_send, wo_recv, wx_recv, wy_recv, wc_recv, far,
):
    users, rows, width = cand.shape
    hist = kv.shape[1]
    inner = wq.shape[1]
    g, s, u = lax.axis_index("grp"), lax.axis_index("seq"), lax.axis_index("usr")
    odd = lax.rem(u, 2)
    partner = u + 1 - 2 * odd
    across = lax.rem(u + 2, 4)
    across_partner = lax.rem(partner + 2, 4)
    step = 1 - 2 * odd
    place = s + odd * (seqs - 1 - 2 * s)

    def user_of(m):
        return m + odd * (users - 1 - 2 * m)

    def block_of(b):
        return b + odd * (seqs - 1 - 2 * b)

    def at_place(b):
        return (g, block_of(b), u)

    variants = [(c, k) for c in range(2) for k in range(seqs)]
    variant = odd * seqs + place

    def pick(choices):
        if len(set(choices)) == 1:
            return choices[0]
        value = choices[-1]
        for v in range(len(choices) - 1):
            value = jnp.where(variant == v, choices[v], value)
        return value

    def by_variant(do):
        for v, (c, k) in enumerate(variants):
            @pl.when(variant == v)
            def _():
                do(c, k)

    loads = {}
    for index, (name, source, target) in enumerate((
        ("cand", cand_hbm, cand), ("wq", wq_hbm, wq), ("lens", len_hbm, lens), ("kv", kv_hbm, kv), ("wg", wg_hbm, wg),
        ("tm", tm_hbm, tm.at[s]), ("wo", wo_hbm, wo), ("wu", wu_hbm, wu.at[u]), ("wd", wd_hbm, wd.at[u]),
    )):
        loads[name] = pltpu.make_async_copy(source, target, load_sem.at[index])

    for name in ("cand", "wq", "lens"):
        loads[name].start()

    barrier = pltpu.get_barrier_semaphore()
    near = [(g, s, partner), (g, s, across), (1 - g, s, u)]
    for peer in near:
        pl.semaphore_signal(barrier, inc=1, device_id=peer, device_id_type=MESH)

    @pl.when(s > 0)
    def _():
        pl.semaphore_signal(barrier, inc=1, device_id=(g, s - 1, u), device_id_type=MESH)

    @pl.when(s < seqs - 1)
    def _():
        pl.semaphore_signal(barrier, inc=1, device_id=(g, s + 1, u), device_id_type=MESH)

    def remote(source, target, send, recv, device):
        return pltpu.make_async_remote_copy(
            src_ref=source, dst_ref=target, send_sem=send, recv_sem=recv,
            device_id=device, device_id_type=MESH,
        )

    def drain(ref, sem):
        pltpu.make_async_copy(ref, ref, sem).wait()

    weights = ((wu_hbm, wu), (wd_hbm, wd))

    def rows_of(piece, half):
        size = weights[piece // PIECES][1].shape[1] // (2 * PIECES)
        return pl.ds(pl.multiple_of((half * PIECES + piece % PIECES) * size, size), size)

    def piece_of(piece, slot, half):
        return weights[piece // PIECES][1].at[slot, rows_of(piece, half)]

    def to_partner_own(w):
        return remote(weights[w][0], weights[w][1].at[u], w_send.at[w], wo_recv.at[w], (g, s, partner))

    def to_across(piece, slot):
        w = piece // PIECES
        source = weights[w][0].at[rows_of(piece, g)]
        return remote(source, piece_of(piece, slot, g), w_send.at[w], wx_recv.at[piece], (g, s, across))

    def to_group(piece, half):
        part = piece_of(piece, across, half)
        return remote(part, part, w_send.at[piece // PIECES], wy_recv.at[piece], (1 - g, s, u))

    def to_partner_far(piece, half):
        part = piece_of(piece, across, half)
        w = piece // PIECES
        return remote(part, part, w_send.at[w], wc_recv.at[w], (g, s, partner))

    def across_arrived(piece):
        to_across(piece, across).wait_recv()
        if piece + DEPTH < 2 * PIECES:
            to_across(piece + DEPTH, u).start()
        to_group(piece, g).start()
        to_partner_far(piece, g).start()

    def group_arrived(piece):
        to_group(piece, 1 - g).wait_recv()
        to_partner_far(piece, 1 - g).start()

    def query_copy(m, b, to):
        ref = queries.at[m, b]
        return remote(ref, ref, q_send, q_recv.at[m, b], at_place(to))

    def early(c, k):
        kinds = [t // 1000 for t in PLAN[c][k]]
        ahead = [t for t in PLAN[c][k][:kinds.index(ATTEND)] if t // 1000 == PASS]
        return [t for t in ahead if numbers_of(t)[:2] == (QUERY_ORDER[c][k][0], k) and abs(t % 10 - k) == 1]

    def pass_queries(m, b, to):
        query_copy(m, b, to).start()

    def send_early(c, k):
        for t in early(c, k):
            pass_queries(*numbers_of(t))

    orders = [QUERY_ORDER[c][k] for c, k in variants]
    first, second = pick([o[0] for o in orders]), pick([o[1] for o in orders])
    loads["cand"].wait()
    loads["wq"].wait()
    loads["kv"].start()
    queries[first, place] = dot(cand[user_of(first)], wq[...]).astype(BF16)
    neighbours = (s > 0).astype(jnp.int32) + (s < seqs - 1).astype(jnp.int32)
    pl.semaphore_wait(barrier, len(near) + neighbours)
    by_variant(send_early)
    for piece in range(DEPTH):
        to_across(piece, u).start()
    for way in (-1, 1):
        @pl.when((s + way >= 0) & (s + way < seqs))
        def _():
            pl.semaphore_signal(far, inc=1, device_id=(g, s + way, u), device_id_type=MESH)

    queries[second, place] = dot(cand[user_of(second)], wq[...]).astype(BF16)
    for name in ("wg", "tm"):
        loads[name].start()

    half_scale = 0.5 / math.sqrt(DH)

    def attend(m, b):
        user = user_of(m)
        for head in range(HEADS):
            cols = slice(head * DH, (head + 1) * DH)
            scores = lax.dot_general(
                queries[m, b, :, cols], kv[user, :, cols], (((1,), (1,)), ((), ())),
                preferred_element_type=F32,
            )
            weight = silu_of_double(scores * half_scale).astype(BF16)
            sums[m, b, :, cols] = dot(weight, values[user, :, cols])

    lane_start = [sum(lanes_of(j) for j in range(m)) for m in range(users)]

    def sum_copy(c, source, m, b, to):
        lane = lane_start[m] + children(c, to, m, b).index(source)
        return remote(
            outgoing.at[m, b], incoming.at[lane * seqs + b], p_send, p_recv.at[lane, b], at_place(to)
        )

    def gather_sum(c, k, m, b):
        total = sums[m, b]
        for child in children(c, k, m, b):
            copy = sum_copy(c, child, m, b, k)
            copy.wait_recv()
            lane = lane_start[m] + children(c, k, m, b).index(child)
            total = total + incoming[lane * seqs + b].astype(F32)
        return total

    def send_sum(c, k, m, b, to):
        outgoing[m, b] = gather_sum(c, k, m, b).astype(BF16)
        sum_copy(c, k, m, b, to).start()

    def sum_complete(c, k, m, b):
        first_row = pl.multiple_of(block_of(b) * rows, rows)
        normed[pl.ds(first_row, rows)] = layer_norm(gather_sum(c, k, m, b)).astype(BF16)

    chip = lax.div(u, 2)
    quarter = rows // 4

    def quarter_rows(group, near_chip):
        return pl.ds(pl.multiple_of((group * 2 + near_chip) * quarter, quarter), quarter)

    def send_mix(k):
        mine = quarter_rows(g, chip)
        remote(tm_hbm.at[mine], tm.at[s, mine], t_send, t_recv.at[0], at_place(1)).start()

    def mix_arrived(turn):
        drain(tm.at[pl.ds(0, seqs - 1), pl.ds(0, quarter)], t_recv.at[turn])

    def pass_mix():
        mix_arrived(0)
        part = tm.at[pl.ds(1 - odd, seqs - 1), quarter_rows(g, chip)]
        remote(part, part, t_send, t_recv.at[0], at_place(0)).start()

    def mix_share(k, near_chip, turn):
        for b in range(seqs):
            if b != k:
                part = tm.at[block_of(b), quarter_rows(g, near_chip)]
                device = (g, s, across) if turn == 1 else (1 - g, s, u)
                remote(part, part, f_send, t_recv.at[turn], device).start()

    def share_first(k):
        if k == 0:
            mix_arrived(0)
        mix_share(k, chip, 1)
        mix_share(k, chip, 2)

    def share_second(k):
        mix_arrived(1)
        mix_share(k, 1 - chip, 3)

    def mixed_copy(to, m):
        return remote(mixed_out.at[to], mixed_in.at[m], m_send, m_recv.at[m], at_place(to))

    def premix(c, k):
        last_row = pl.multiple_of(block_of(steps_of(c, k, COMPLETE)[-1][1]) * rows, rows)
        normed[pl.ds(last_row, rows)] = jnp.zeros((rows, inner), BF16)
        mix_arrived(2)
        mix_arrived(3)
        for b in range(seqs):
            first_row = pl.multiple_of(block_of(b) * rows, rows)
            mixed_sum[b] = normed[pl.ds(first_row, rows)].astype(F32) + dot(tm[block_of(b)], normed[...])

    def mix(c, k):
        last = steps_of(c, k, COMPLETE)[-1][1]
        last_rows = pl.ds(pl.multiple_of(block_of(last) * rows, rows), rows)
        late = normed[last_rows]
        for b in sorted(range(seqs), key=lambda b: -abs(b - k)):
            mixed = mixed_sum[b] + dot(tm[block_of(b), :, last_rows], late)
            if b == last:
                mixed = mixed + late.astype(F32)
            if b == k:
                mixed_in[k] = mixed.astype(BF16)
            else:
                mixed_out[b] = mixed.astype(BF16)
                mixed_copy(b, k).start()

    def act(c, k, step):
        kind, (m, b, to) = step // 1000, numbers_of(step)
        if kind == PASS:
            pass_queries(m, b, to)
        elif kind == ARRIVED:
            query_copy(m, b, k).wait_recv()
        elif kind == SEND_SUM:
            send_sum(c, k, m, b, to)
        elif kind == COMPLETE:
            sum_complete(c, k, m, b)
        elif kind == PIECE_ACROSS:
            across_arrived(step % 100)
        elif kind == PIECE_GROUP:
            group_arrived(step % 100)
        elif kind == SEND_MIX:
            send_mix(k)
        elif kind == PASS_MIX:
            pass_mix()
        elif kind == PREMIX:
            premix(c, k)
        elif kind == MIX:
            mix(c, k)
        elif kind == SHARE_FIRST:
            share_first(k)
        elif kind == SHARE_SECOND:
            share_second(k)

    def run(c, k, steps):
        for step in steps:
            act(c, k, step)

    parts = []
    for c, k in variants:
        parts.append([[]])
        skipped = early(c, k)
        for t in PLAN[c][k]:
            if t not in skipped:
                parts[-1][-1].append(t)
            if t // 1000 == ATTEND:
                parts[-1].append([])
    for index in range(users * seqs):
        by_variant(lambda c, k: run(c, k, parts[c * seqs + k][index][:-1]))
        if index == 0:
            loads["lens"].wait()
            loads["kv"].wait()
            for m in range(users):
                slots = s * hist + lax.broadcasted_iota(jnp.int32, (hist, 1), 0)
                visible = jnp.where(slots < lens[m], 1.0, 0.0)
                values[m] = (kv[m, :, inner:].astype(F32) * visible).astype(BF16)
        chosen = [numbers_of(part[index][-1]) for part in parts]
        attend(pick([n[0] for n in chosen]), pick([n[1] for n in chosen]))
        if index == 0:
            pl.semaphore_wait(far, neighbours)
            loads["wg"].wait()
            loads["tm"].wait()
            for m in range(users):
                gates[m] = silu_of_double(dot(cand[user_of(m)], wg[...]) * 0.5)
        if index == LATE_LOADS:
            for w in range(2):
                to_partner_own(w).start()
            for name in ("wo", "wu", "wd"):
                loads[name].start()
    by_variant(lambda c, k: run(c, k, parts[c * seqs + k][-1]))

    loads["wo"].wait()
    slots = (u, partner, across, across_partner)
    for index in range(users):
        m = pick([TAIL_ORDER[c][k][index] for c, k in variants])

        @pl.when(place != m)
        def _():
            mixed_copy(place, m).wait_recv()

        user = user_of(m)
        gated = (mixed_in[m].astype(F32) * gates[m]).astype(BF16)
        state = cand[user].astype(F32) + dot(gated, wo[...])
        states[...] = state
        ffn_in = layer_norm(state).astype(BF16)
        if index == 0:
            loads["wu"].wait()
            remote(wu_hbm, wu.at[partner], w_send.at[0], wo_recv.at[0], (g, s, partner)).wait_recv()
            drain(wu.at[across_partner], wc_recv.at[0])
        hidden = [gelu_tanh(dot(ffn_in, wu[slot])).astype(BF16) for slot in slots]
        if index == 0:
            loads["wd"].wait()
            remote(wd_hbm, wd.at[partner], w_send.at[1], wo_recv.at[1], (g, s, partner)).wait_recv()
            drain(wd.at[across_partner], wc_recv.at[1])
        for start in range(0, width, COLUMNS):
            cols = slice(start, min(start + COLUMNS, width))
            total = states[:, cols]
            for h, slot in zip(hidden, slots):
                total = total + dot(h, wd[slot, :, cols])
            out_ref[user, :, cols] = total.astype(BF16)

    def finish(c, k):
        def blocks(kind):
            return incoming.at[pl.ds(0, len(steps_of(c, k, kind)))]

        drain(blocks(PASS), q_send)
        drain(blocks(SEND_SUM), p_send)
        drain(tm.at[pl.ds(0, seqs - 1 if k == 1 else 1), pl.ds(0, quarter)], t_send)
        if k < users:
            drain(tm.at[pl.ds(0, seqs - 1), pl.ds(0, 3 * quarter)], f_send)
            drain(incoming.at[pl.ds(0, seqs - 1)], m_send)

    by_variant(finish)
    drain(wu.at[pl.ds(0, 3)], w_send.at[0])
    drain(wd.at[pl.ds(0, 3)], w_send.at[1])


def fused(seqs, usrs, history_kv, candidates, lengths, w_query, w_gate, token_mix, w_out, w_up, w_down):
    users, hist, _ = history_kv.shape
    rows, width = candidates.shape[1:]
    inner = w_query.shape[1]
    depth = w_up.shape[1]
    dma = pltpu.SemaphoreType.DMA
    hbm = pl.BlockSpec(memory_space=pltpu.HBM)
    lanes = sum(lanes_of(m) for m in range(users))
    operands = (history_kv, candidates, lengths, w_query, w_gate, token_mix, w_out, w_up, w_down)
    return pl.pallas_call(
        functools.partial(kernel, seqs),
        out_shape=jax.ShapeDtypeStruct(candidates.shape, BF16),
        in_specs=[hbm] * len(operands),
        out_specs=pl.BlockSpec(memory_space=pltpu.VMEM),
        scratch_shapes=[
            pltpu.VMEM(history_kv.shape, BF16),
            pltpu.VMEM(candidates.shape, BF16),
            pltpu.VMEM(w_query.shape, BF16),
            pltpu.VMEM(w_gate.shape, BF16),
            pltpu.VMEM((seqs, *token_mix.shape), BF16),
            pltpu.VMEM(w_out.shape, BF16),
            pltpu.VMEM((usrs, width, depth), BF16),
            pltpu.VMEM((usrs, depth, width), BF16),
            pltpu.VMEM((users, hist, inner), BF16),
            pltpu.VMEM((users, seqs, rows, inner), BF16),
            pltpu.VMEM((users, seqs, rows, inner), F32),
            pltpu.VMEM((users, seqs, rows, inner), BF16),
            pltpu.VMEM((lanes * seqs, rows, inner), BF16),
            pltpu.VMEM((seqs * rows, inner), BF16),
            pltpu.VMEM((seqs, rows, inner), F32),
            pltpu.VMEM((seqs, rows, inner), BF16),
            pltpu.VMEM((users, rows, inner), BF16),
            pltpu.VMEM((users, rows, inner), F32),
            pltpu.VMEM((rows, width), F32),
            pltpu.SMEM(lengths.shape, jnp.int32),
            dma((9,)),
            dma, dma((users, seqs)), dma, dma((lanes, seqs)),
            dma, dma((4,)), dma, dma, dma((users,)),
            dma((2,)), dma((2,)), dma((2 * PIECES,)), dma((2 * PIECES,)), dma((2,)),
            pltpu.SemaphoreType.REGULAR,
        ],
        compiler_params=pltpu.CompilerParams(
            collective_id=0, has_side_effects=True, vmem_limit_bytes=34 * 1024 * 1024
        ),
        name="rank_layer",
    )(*(pltpu.with_memory_space_constraint(operand, pltpu.HBM) for operand in operands))


def shards(history_kv, candidates, lengths, w_query, w_gate, token_mix, w_out, w_up, w_down):
    user_count, hist_dev, _ = history_kv.shape
    inner = w_query.shape[1]
    half = hist_dev // 2
    scale = 1.0 / math.sqrt(DH)
    seq_index = lax.axis_index("seq")
    first_start = seq_index * hist_dev
    sections = ((history_kv[:, :half], first_start), (history_kv[:, half:], first_start + half))
    offsets = lax.iota(jnp.int32, half)
    queries = jnp.einsum(
        "ucd,de->uce", candidates, w_query, preferred_element_type=jnp.float32
    ).astype(jnp.bfloat16)
    piece = lax.all_gather(queries, "seq", axis=1, tiled=True)
    row_count = piece.shape[1]
    results = []
    for member in range(user_count):
        query_heads = piece[member].reshape(row_count, HEADS, DH)
        limit = lengths[member]
        summed = jnp.zeros((row_count, inner), jnp.float32)
        for section, section_start in sections:
            key_heads = section[member, :, :inner].reshape(half, HEADS, DH)
            value_heads = section[member, :, inner:].reshape(half, HEADS, DH)

            def compute(
                operand,
                key_heads=key_heads,
                value_heads=value_heads,
                section_start=section_start,
                query_heads=query_heads,
                limit=limit,
            ):
                scores = (
                    jnp.einsum(
                        "chd,thd->hct", query_heads, key_heads, preferred_element_type=jnp.float32
                    )
                    * scale
                )
                visible = section_start + offsets < limit
                weights = jnp.where(visible[None, None, :], jax.nn.silu(scores), 0.0).astype(
                    jnp.bfloat16
                )
                contrib = jnp.einsum(
                    "hct,thd->chd", weights, value_heads, preferred_element_type=jnp.float32
                )
                return contrib.reshape(row_count, inner)

            def skipped(operand):
                return jnp.zeros((row_count, inner), jnp.float32)

            summed = summed + lax.cond(section_start < limit, compute, skipped, 0)
        results.append(summed)
    partial_sums = jnp.stack(results)
    attended = lax.psum_scatter(partial_sums, "seq", scatter_dimension=1, tiled=True)
    normed = layer_norm(attended).astype(jnp.bfloat16)
    mixed = normed.astype(jnp.float32) + jnp.einsum(
        "cp,upe->uce",
        token_mix,
        lax.all_gather(normed, "seq", axis=1, tiled=True),
        preferred_element_type=jnp.float32,
    )
    gate_values = jax.nn.silu(
        jnp.einsum("ucd,de->uce", candidates, w_gate, preferred_element_type=jnp.float32)
    )
    gated = (mixed * gate_values).astype(jnp.bfloat16)
    state = candidates.astype(jnp.float32) + jnp.einsum(
        "uce,ed->ucd", gated, w_out, preferred_element_type=jnp.float32
    )
    ffn_in = layer_norm(state).astype(jnp.bfloat16)
    hidden = jax.nn.gelu(
        jnp.einsum(
            "ucd,df->ucf",
            lax.all_gather(ffn_in, "usr", axis=0, tiled=True),
            w_up,
            preferred_element_type=jnp.float32,
        )
    ).astype(jnp.bfloat16)
    ffn_terms = jnp.einsum("ucf,fd->ucd", hidden, w_down, preferred_element_type=jnp.float32)
    ffn_out = lax.psum_scatter(
        ffn_terms.astype(jnp.bfloat16), "usr", scatter_dimension=0, tiled=True
    ).astype(jnp.float32)
    return (state + ffn_out).astype(jnp.bfloat16)


def solution(mesh):
    sizes = dict(mesh.shape)
    seqs, usrs = sizes["seq"], sizes["usr"]
    def body(history_kv, candidates, *rest):
        operands = (history_kv, candidates, *rest)
        fits = sizes["grp"] == 2 and usrs == 4 and seqs == len(PLAN[0])
        if fits and candidates.shape[0] == len(QUERY_ORDER[0][0]):
            return fused(seqs, usrs, *operands)
        return shards(*operands)

    return jax.shard_map(
        body,
        mesh=mesh,
        in_specs=(
            P(("grp", "usr"), "seq", None),
            P(("grp", "usr"), "seq", None),
            P(("grp", "usr")),
            P(),
            P(),
            P("seq", None),
            P(),
            P(None, "usr"),
            P("usr", None),
        ),
        out_specs=P(("grp", "usr"), "seq", None),
        check_vma=False,
    )
```
